32 devices in a mesh: grp: 2 (over x), row: 16 (over z, y, core).
Axes of the slice: x: 2, y: 2, z: 4, core: 2. Of those that a mesh axis runs over, the one named last changes fastest.
Arguments:
- field: bfloat16 [256, 1024, 256], P(('grp', 'row')), parts along dimension 0, may hold values from -8 to 8, as said below
- w_qkv: bfloat16 [256, 768], replicated, may hold values from -0.375 to 0.375
- w_attn: bfloat16 [256, 256], replicated, may hold values from -0.375 to 0.375
- w_inner: bfloat16 [256, 512], replicated, may hold values from -0.375 to 0.375
- w_outer: bfloat16 [512, 256], replicated, may hold values from -0.25 to 0.25
- w_skip: bfloat16 [256, 256], replicated, may hold values from -0.375 to 0.375
- w_modes: bfloat16 [512, 2, 256, 256], P('row'), may hold values from -0.25 to 0.25
Outputs:
- result: bfloat16 [256, 1024, 256], P(('grp', 'row')), parts along dimension 0
The draws below stay inside these ranges and needn't reach their ends.
There are 2 independent parts, one for each index of `grp`. The reference program is written for one: setup_inputs(seed, part) draws one part's arguments, and reference() takes and returns one part's arrays. A program takes and returns all parts, laid end to end along the dimension named above; an argument that names none is the same for every part. Nothing has to cross between parts.
Inputs may be any that keep to these rules, and one draw needn't show every extreme that they name: `field`: features of the slab's cells.
All inputs are finite; a program needn't handle non-finite values.
Results may differ from the reference program's by a relative error of at most 0.004.
The reference program's roundings to bfloat16 on the way (of `scaled_kv`, `attended`, `first`, `hidden`, `second`, `coeff_b`, `mixed` and `back`) count: a program that leaves them out, or rounds other values in their place, can miss the bound.
Values may be sent and summed in bfloat16 or wider, within the bound.
No kernel may reach another device: no remote copies, remote signals or barrier semaphores. Data moves between devices by JAX's collectives and lax.ppermute only.
A program may use at most 128 MiB of HBM per device.

```python
import jax
import jax.numpy as jnp
from jax import lax

HEADS = 4
HD = 64
C = 256
FF = 512
W = 1024
MH = 32
MW = 16
NROWS = 128
MODES = 512


def draw_field(key, part):
    base_key = jax.random.fold_in(key, 7)
    noise_key, pattern_key = jax.random.split(base_key, 2)
    row_pos = jnp.arange(NROWS, dtype=jnp.float32) / max(NROWS - 1, 1)
    ramp_rows = 0.3 + 0.6 * row_pos
    col_pos = jnp.arange(W, dtype=jnp.float32) / W
    across_cols = 1.0 + 0.5 * jnp.cos(6.283185307179586 * col_pos)
    pattern_vec = jax.random.normal(pattern_key, (C,), jnp.float32)
    noise_field = jax.random.normal(noise_key, (NROWS, W, C), jnp.float32)
    result_field = noise_field + ramp_rows[:, None, None] * across_cols[None, :, None] * pattern_vec[None, None, :]
    return jnp.clip(result_field, -8.0, 8.0).astype(jnp.bfloat16)


def level_of(rng, dims, shards, smallest, largest):
    def one(axis_at, parts):
        steps = jax.random.uniform(jax.random.fold_in(jax.random.fold_in(rng, 6), axis_at), (parts,), jnp.float32, smallest / len(shards), largest / len(shards))
        return jnp.repeat(jnp.exp(steps), dims[axis_at] // parts).reshape((-1,) + (1,) * (len(dims) - axis_at - 1))

    factor_of = one(*shards[0])
    for cut in shards[1:]:
        factor_of = factor_of * one(*cut)
    return factor_of


def gaussian(stream_key, shape, deviation, most, cuts=(), held_as=jnp.bfloat16):
    gain = level_of(stream_key, shape, cuts, -0.22, 0.18) if cuts else 1.0
    entries = jax.random.normal(stream_key, shape, jnp.float32) * deviation * gain
    return jnp.minimum(jnp.maximum(entries, -most), most).astype(held_as)


def setup_inputs(seed: int = 0, part: int = 0) -> dict:
    key_list = jax.random.split(jax.random.key(seed), 8)
    part_splits = jax.random.split(jax.random.fold_in(key_list[7], part), 8)
    return {
        "field": draw_field(jax.random.fold_in(jax.random.fold_in(key_list[7], part), 71), part),
        "w_qkv": gaussian(key_list[1], (C, 3 * C), C ** -0.5, 0.375),
        "w_attn": gaussian(key_list[2], (C, C), C ** -0.5, 0.375),
        "w_inner": gaussian(key_list[3], (C, FF), C ** -0.5, 0.375),
        "w_outer": gaussian(key_list[4], (FF, C), FF ** -0.5, 0.25),
        "w_skip": gaussian(key_list[5], (C, C), C ** -0.5, 0.375),
        "w_modes": gaussian(key_list[6], (MODES, 2, C, C), (2 * C) ** -0.5, 0.25, ((0, 16),)),
    }


EPSILON = 1e-05
TWO_PI = 6.283185307179586

def head_norm(blocked, heads):
    shaped = blocked.reshape(blocked.shape[0], heads, -1)
    center = shaped - lax.optimization_barrier(jnp.mean(shaped, axis=-1, keepdims=True))
    spread = lax.optimization_barrier(jnp.mean(center * center, axis=-1, keepdims=True))
    return (center * lax.rsqrt(spread + EPSILON)).astype(jnp.bfloat16)

def column_table(columns, modes):
    col_index = jnp.arange(columns, dtype=jnp.int32)
    freqs = jnp.arange(modes, dtype=jnp.int32)
    turns = freqs[:, None] * col_index[None, :] % columns
    angle = turns.astype(jnp.float32) * (TWO_PI / columns)
    return (jnp.cos(angle), jnp.sin(angle))

def row_angles(height, modes, rows_global):
    freqs = jnp.arange(modes, dtype=jnp.int32)
    signed = jnp.where(freqs < modes // 2, freqs, freqs - modes + height)
    turns = signed[:, None] * rows_global[None, :] % height
    angle = turns.astype(jnp.float32) * (TWO_PI / height)
    return (jnp.cos(angle), jnp.sin(angle))

def reference(field, w_qkv, w_attn, w_inner, w_outer, w_skip, w_modes):
    height, columns, channels = field.shape
    highest = lax.Precision.HIGHEST
    tokens = field.reshape(-1, channels)
    projected = jnp.dot(tokens, w_qkv, preferred_element_type=jnp.float32)
    queries = projected[:, :channels].astype(jnp.bfloat16).reshape(-1, HEADS, HD)
    key_rows = head_norm(projected[:, channels:2 * channels], HEADS)
    value_rows = head_norm(projected[:, 2 * channels:], HEADS)
    summed_kv = jnp.einsum('thd,the->hde', key_rows.astype(jnp.float32), value_rows.astype(jnp.float32))
    scaled_kv = (summed_kv / (height * columns)).astype(jnp.bfloat16)
    attended = jnp.einsum('thd,hde->the', queries.astype(jnp.float32), scaled_kv.astype(jnp.float32))
    attended = attended.astype(jnp.bfloat16).reshape(-1, channels)
    first = (tokens.astype(jnp.float32) + jnp.dot(attended, w_attn, preferred_element_type=jnp.float32)).astype(jnp.bfloat16)
    hidden = jax.nn.gelu(jnp.dot(first, w_inner, preferred_element_type=jnp.float32), approximate=False).astype(jnp.bfloat16)
    second = (first.astype(jnp.float32) + jnp.dot(hidden, w_outer, preferred_element_type=jnp.float32)).astype(jnp.bfloat16)
    slab_grid = second.reshape(height, columns, channels)
    col_cos, col_sin = column_table(columns, MW)
    forward_tab = jnp.concatenate([col_cos, -col_sin], axis=0).T.astype(jnp.bfloat16)
    row_spectra = jnp.einsum('rwc,wk->rkc', slab_grid.astype(jnp.float32), forward_tab.astype(jnp.float32))
    spec_re = row_spectra[:, :MW]
    spec_im = row_spectra[:, MW:]
    row_cos, row_sin = row_angles(height, MH, jnp.arange(height, dtype=jnp.int32))
    coeff_re = jnp.einsum('hr,rkc->hkc', row_cos, spec_re, precision=highest) + jnp.einsum('hr,rkc->hkc', row_sin, spec_im, precision=highest)
    coeff_im = jnp.einsum('hr,rkc->hkc', row_cos, spec_im, precision=highest) - jnp.einsum('hr,rkc->hkc', row_sin, spec_re, precision=highest)
    coeff_b = jnp.concatenate([coeff_re, coeff_im], axis=-1).reshape(MH * MW, 2 * channels).astype(jnp.bfloat16)
    coeff_f = coeff_b.astype(jnp.float32)
    mode_re = w_modes[:, 0].astype(jnp.float32)
    mode_im = w_modes[:, 1].astype(jnp.float32)
    part_re = coeff_f[:, :channels]
    part_im = coeff_f[:, channels:]
    mixed_re = jnp.einsum('mc,mco->mo', part_re, mode_re) - jnp.einsum('mc,mco->mo', part_im, mode_im)
    mixed_im = jnp.einsum('mc,mco->mo', part_re, mode_im) + jnp.einsum('mc,mco->mo', part_im, mode_re)
    mixed = jnp.concatenate([mixed_re, mixed_im], axis=-1).astype(jnp.bfloat16)
    mixed_f = mixed.astype(jnp.float32).reshape(MH, MW, 2 * channels)
    out_re = mixed_f[..., :channels]
    out_im = mixed_f[..., channels:]
    back_re = jnp.einsum('hr,hkc->rkc', row_cos, out_re, precision=highest) - jnp.einsum('hr,hkc->rkc', row_sin, out_im, precision=highest)
    back_im = jnp.einsum('hr,hkc->rkc', row_cos, out_im, precision=highest) + jnp.einsum('hr,hkc->rkc', row_sin, out_re, precision=highest)
    weights_kw = jnp.where(jnp.arange(MW, dtype=jnp.int32) == 0, 1.0, 2.0).astype(jnp.float32) / (height * columns)
    back = (jnp.concatenate([back_re, back_im], axis=-1) * weights_kw[None, :, None]).astype(jnp.bfloat16)
    back_stack = jnp.concatenate([back[..., :channels], back[..., channels:]], axis=1)
    inverse_tab = jnp.concatenate([col_cos, -col_sin], axis=0).astype(jnp.bfloat16)
    spectral = jnp.einsum('rkc,kw->rwc', back_stack.astype(jnp.float32), inverse_tab.astype(jnp.float32))
    skipped = jnp.dot(second, w_skip, preferred_element_type=jnp.float32)
    result = jax.nn.gelu(skipped + spectral.reshape(-1, channels), approximate=False)
    return result.astype(jnp.bfloat16).reshape(height, columns, channels)
```

```python
import functools

import jax
import jax.numpy as jnp
import numpy as np
from jax import lax
from jax.experimental import pallas as pl
from jax.experimental.pallas import tpu as pltpu
from jax.sharding import PartitionSpec as P

HEADS = 4
HD = 64
MH = 32
MW = 16
EPSILON = 1e-05
SUB = 256
F32 = jnp.float32
BF16 = jnp.bfloat16


def mm(a, b):
    return jnp.dot(a, b, preferred_element_type=F32)


def mm_nt(a, b):
    return lax.dot_general(a, b, (((1,), (1,)), ((), ())), preferred_element_type=F32)


def gelu(x):
    half = 0.5 * x
    return half + half * lax.erf(x * 0.7071067811865476)


def bit_reverse(value, bits):
    out = 0
    for b in range(bits):
        out |= ((value >> b) & 1) << (bits - 1 - b)
    return out


def column_table(columns):
    turns = np.arange(columns)[:, None] * np.arange(MW)[None, :] % columns
    angle = turns * (2 * np.pi / columns)
    return np.concatenate([np.cos(angle), -np.sin(angle)], axis=1)


def row_table(height, strip_rows):
    freqs = np.arange(MH // 2 + 1)
    turns = freqs[None, :, None] * np.arange(height).reshape(-1, 1, strip_rows) % height
    angle = turns * (2 * np.pi / height)
    both = np.concatenate([np.cos(angle), np.sin(angle)], axis=1)
    return both.reshape(both.shape[0], 1, -1).astype(np.float32)


def pieces(kh, per_owner):
    count = min(MW, per_owner)
    for first in range(0, MW, count):
        mode = kh * MW + first
        yield mode // per_owner, mode % per_owner, first, count


def kv_kernel(x_ref, w_ref, out_ref, w_t, acc):
    step = pl.program_id(0)
    channels = HEADS * HD

    @pl.when(step == 0)
    def _():
        w_t[...] = w_ref[...].T
        acc[...] = jnp.zeros_like(acc)

    total = acc[...]
    for at in range(0, x_ref.shape[0], SUB):
        x = x_ref[at : at + SUB, :]
        both = mm_nt(w_t[channels:, :], x)
        shaped = both.reshape(2 * HEADS, HD, SUB)
        center = shaped - jnp.sum(shaped, axis=1, keepdims=True) * (1.0 / HD)
        spread = jnp.sum(center * center, axis=1, keepdims=True) * (1.0 / HD) + EPSILON
        scale = lax.rsqrt(spread[:HEADS]) * lax.rsqrt(spread[HEADS:])
        keys = (center[:HEADS] * scale).reshape(channels, SUB).astype(BF16)
        values = center[HEADS:].reshape(channels, SUB).astype(BF16)
        total = total + mm_nt(keys, values)
    acc[...] = total

    @pl.when(step == pl.num_programs(0) - 1)
    def _():
        left = lax.broadcasted_iota(jnp.int32, (HD, 2 * HD), 1) < HD
        for pair in range(HEADS // 2):
            row = 2 * pair * HD
            cols = slice(row, row + 2 * HD)
            out_ref[pair * HD : (pair + 1) * HD, :] = jnp.where(
                left, total[row : row + HD, cols], total[row + HD : row + 2 * HD, cols]
            )


def field_kernel(cells, me_ref, x_ref, kva_ref, kvb_ref, wq_ref, wa_ref, wi_ref, wo_ref, tab_ref, ang_ref,
                 second_ref, keep_ref, send_ref, scaled, spectra, terms):
    step = pl.program_id(0)
    channels = HEADS * HD
    rows = spectra.shape[0]

    @pl.when(step == 0)
    def _():
        packed = (kva_ref[...] + kvb_ref[...]) / cells
        left = lax.broadcasted_iota(jnp.int32, (HD, 2 * HD), 1) < HD
        blank = jnp.zeros((HD, 2 * HD), F32)
        blocks = []
        for pair in range(HEADS // 2):
            part = packed[pair * HD : (pair + 1) * HD, :]
            for mine in (jnp.where(left, part, 0.0), jnp.where(left, 0.0, part)):
                line = [blank] * (HEADS // 2)
                line[pair] = mine
                blocks.append(jnp.concatenate(line, axis=1))
        scaled[...] = jnp.concatenate(blocks, axis=0).astype(BF16)

    for at in range(0, x_ref.shape[0], SUB):
        x = x_ref[at : at + SUB, :]
        queries = mm(x, wq_ref[...]).astype(BF16)
        attended = mm(queries, scaled[...]).astype(BF16)
        first = (x.astype(F32) + mm(attended, wa_ref[...])).astype(BF16)
        hidden = gelu(mm(first, wi_ref[...])).astype(BF16)
        second_ref[at : at + SUB, :] = (first.astype(F32) + mm(hidden, wo_ref[...])).astype(BF16)
    spectra[step] = mm(tab_ref[...], second_ref[...])

    @pl.when(step == pl.num_programs(0) - 1)
    def _():
        owners, per_owner, _ = terms.shape
        bits = owners.bit_length() - 1
        for f in range(MH // 2 + 1):
            parts = [jnp.zeros((MW, channels), F32)] * 4
            for r in range(rows):
                cos = ang_ref[0, 0, f * rows + r]
                sin = ang_ref[0, 0, (MH // 2 + 1 + f) * rows + r]
                re = spectra[r, :MW, :]
                im = spectra[r, MW:, :]
                parts = [parts[0] + cos * re, parts[1] + cos * im, parts[2] + sin * re, parts[3] + sin * im]
            cr, ci, sr, si = parts
            found = []
            if f < MH // 2:
                found.append((f, cr + si, ci - sr))
            if f > 0:
                found.append((MH - f, cr - si, ci + sr))
            for kh, re, im in found:
                for owner, row, kw, count in pieces(kh, per_owner):
                    at = bit_reverse(owner, bits) ^ me_ref[0]
                    terms[at, row : row + count, :channels] = re[kw : kw + count]
                    terms[at, row : row + count, channels:] = im[kw : kw + count]
        keep_ref[...] = terms[: owners // 2]
        send_ref[...] = terms[owners // 2 :].astype(BF16)


def mode_kernel(keep_ref, recv_ref, w_ref, out_ref):
    step = pl.program_id(0)
    group = w_ref.shape[0]
    channels = HEADS * HD
    rows = pl.ds(pl.multiple_of(step * group, group), group)
    coeff = (keep_ref[rows, :] + recv_ref[rows, :].astype(F32)).astype(BF16).astype(F32)
    re, im = coeff[:, :channels], coeff[:, channels:]
    lhs = jnp.concatenate(
        [jnp.concatenate([re, -im], axis=1), jnp.concatenate([im, re], axis=1)], axis=0
    ).astype(BF16)
    index = lax.broadcasted_iota(jnp.int32, (2 * group, channels), 0) % group
    mixed = jnp.zeros((2 * group, channels), F32)
    for m in range(group):
        mixed = jnp.where(index == m, mm(lhs, w_ref[m]), mixed)
    out_ref[:, :channels] = mixed[:group].astype(BF16)
    out_ref[:, channels:] = mixed[group:].astype(BF16)


def last_kernel(cells, me_ref, second_ref, lo_ref, hi_ref, ws_ref, tab_ref, ang_ref, out_ref, mixed, sums, diffs):
    step = pl.program_id(0)
    channels = HEADS * HD
    rows = pl.num_programs(0)
    half = MH // 2

    @pl.when(step == 0)
    def _():
        owners, per_owner, _ = mixed.shape
        bits = owners.bit_length() - 1
        mixed[: owners // 2] = lo_ref[...].astype(F32)
        mixed[owners // 2 :] = hi_ref[...].astype(F32)

        def read(kh):
            found = []
            for owner, row, _, count in pieces(kh, per_owner):
                at = bit_reverse(owner, bits) ^ me_ref[0]
                found.append(mixed[at, row : row + count, :])
            return found[0] if len(found) == 1 else jnp.concatenate(found, axis=0)

        for f in range(half + 1):
            if f == 0:
                plus = read(0)
                sums[f] = plus
                diffs[f] = plus
            elif f == half:
                minus = read(half)
                sums[f] = minus
                diffs[f] = -minus
            else:
                plus, minus = read(f), read(MH - f)
                sums[f] = plus + minus
                diffs[f] = plus - minus

    re = jnp.zeros((MW, channels), F32)
    im = jnp.zeros((MW, channels), F32)
    for f in range(half + 1):
        cos = ang_ref[0, 0, f * rows + step]
        sin = ang_ref[0, 0, (half + 1 + f) * rows + step]
        re = re + cos * sums[f, :, :channels] - sin * diffs[f, :, channels:]
        im = im + cos * sums[f, :, channels:] + sin * diffs[f, :, :channels]
    kw = lax.broadcasted_iota(jnp.int32, (MW, channels), 0)
    weight = jnp.where(kw == 0, 1.0, 2.0) / cells
    back = jnp.concatenate([re * weight, im * weight], axis=0).astype(BF16)
    for at in range(0, second_ref.shape[0], SUB):
        here = slice(at, at + SUB)
        value = mm(second_ref[here, :], ws_ref[...]) + mm(tab_ref[here, :], back)
        out_ref[here, :] = gelu(value).astype(BF16)


def whole(shape):
    return pl.BlockSpec(shape, lambda *_: (0,) * len(shape))


def local(field, w_qkv, w_attn, w_inner, w_outer, w_skip, w_modes):
    strip_rows, columns, channels = field.shape
    hidden = w_inner.shape[1]
    size = lax.axis_size("row")
    bits = size.bit_length() - 1
    assert size == 1 << bits and size > 1
    me = lax.axis_index("row")
    height = strip_rows * size
    cells = float(height * columns)
    per_owner = w_modes.shape[0]
    turned = jnp.zeros((), jnp.int32)
    for b in range(bits):
        turned = turned | (((me >> b) & 1) << (bits - 1 - b))
    ids = jnp.stack([turned, me]).astype(jnp.int32)

    def swap(value, distance):
        return lax.ppermute(value, "row", [(i, i ^ distance) for i in range(size)])

    table = column_table(columns)
    wide = jnp.asarray(table.T, BF16)
    tall = jnp.asarray(table, BF16)
    angles = jnp.asarray(row_table(height, strip_rows))
    per_row = pl.BlockSpec((None, columns, channels), lambda r, *_: (r, 0, 0))
    angle_spec = pl.BlockSpec((1, 1, angles.shape[2]), lambda r, ids_ref: (ids_ref[1], 0, 0), memory_space=pltpu.SMEM)

    kv = pl.pallas_call(
        kv_kernel,
        out_shape=jax.ShapeDtypeStruct((2 * HD, 2 * HD), F32),
        grid=(strip_rows,),
        in_specs=[per_row, whole(w_qkv.shape)],
        out_specs=whole((2 * HD, 2 * HD)),
        scratch_shapes=[pltpu.VMEM((3 * channels, channels), BF16), pltpu.VMEM((channels, channels), F32)],
        name="kv",
    )(field, w_qkv)
    for b in range(bits - 1):
        kv = kv + swap(kv, 1 << b)
    other = swap(kv, size // 2)

    half = (size // 2, per_owner, 2 * channels)
    second, keep, send = pl.pallas_call(
        functools.partial(field_kernel, cells),
        out_shape=[
            jax.ShapeDtypeStruct(field.shape, BF16),
            jax.ShapeDtypeStruct(half, F32),
            jax.ShapeDtypeStruct(half, BF16),
        ],
        grid_spec=pltpu.PrefetchScalarGridSpec(
            num_scalar_prefetch=1,
            grid=(strip_rows,),
            in_specs=[
                per_row,
                whole(kv.shape),
                whole(kv.shape),
                whole((channels, channels)),
                whole(w_attn.shape),
                whole(w_inner.shape),
                whole(w_outer.shape),
                whole(wide.shape),
                angle_spec,
            ],
            out_specs=[per_row, whole(half), whole(half)],
            scratch_shapes=[
                pltpu.VMEM((channels, channels), BF16),
                pltpu.VMEM((strip_rows, 2 * MW, channels), F32),
                pltpu.VMEM((size, per_owner, 2 * channels), F32),
            ],
        ),
        name="field",
    )(ids, field, kv, other, w_qkv, w_attn, w_inner, w_outer, wide, angles)

    recv = swap(send, 1)
    for b in range(1, bits):
        cut = keep.shape[0] // 2
        keep, send = (
            keep[:cut] + recv[:cut].astype(F32),
            (keep[cut:] + recv[cut:].astype(F32)).astype(BF16),
        )
        recv = swap(send, 1 << b)
    keep, recv = keep[0], recv[0]

    group = 8
    mixed = pl.pallas_call(
        mode_kernel,
        out_shape=jax.ShapeDtypeStruct((per_owner, 2 * channels), BF16),
        grid=(per_owner // group,),
        in_specs=[
            whole(keep.shape),
            whole(recv.shape),
            pl.BlockSpec((group, 2 * channels, channels), lambda m: (m, 0, 0)),
        ],
        out_specs=pl.BlockSpec((group, 2 * channels), lambda m: (m, 0)),
        name="modes",
    )(keep, recv, w_modes.reshape(per_owner, 2 * channels, channels))

    held = mixed[None]
    for b in range(bits - 1, 0, -1):
        held = jnp.concatenate([held, swap(held, 1 << b)], axis=0)
    far = swap(held, 1)

    return pl.pallas_call(
        functools.partial(last_kernel, cells),
        out_shape=jax.ShapeDtypeStruct(field.shape, BF16),
        grid_spec=pltpu.PrefetchScalarGridSpec(
            num_scalar_prefetch=1,
            grid=(strip_rows,),
            in_specs=[
                per_row,
                whole(half),
                whole(half),
                whole(w_skip.shape),
                whole(tall.shape),
                angle_spec,
            ],
            out_specs=per_row,
            scratch_shapes=[
                pltpu.VMEM((size, per_owner, 2 * channels), F32),
                pltpu.VMEM((MH // 2 + 1, MW, 2 * channels), F32),
                pltpu.VMEM((MH // 2 + 1, MW, 2 * channels), F32),
            ],
        ),
        name="last",
    )(ids, second, held, far, w_skip, tall, angles)


def solution(mesh):
    placed = (P(("grp", "row"), None, None), P(), P(), P(), P(), P(), P("row", None, None, None))
    return jax.shard_map(
        local, mesh=mesh, in_specs=placed, out_specs=P(("grp", "row"), None, None), check_vma=False
    )
```

```python
import functools

import jax
import jax.numpy as jnp
import numpy as np
from jax import lax
from jax.experimental import pallas as pl
from jax.experimental.pallas import tpu as pltpu
from jax.sharding import PartitionSpec as P

HEADS = 4
HD = 64
MH = 32
MW = 16
EPSILON = 1e-05
SUB = 256
F32 = jnp.float32
BF16 = jnp.bfloat16


def mm(a, b):
    return jnp.dot(a, b, preferred_element_type=F32)


def mm_nt(a, b):
    return lax.dot_general(a, b, (((1,), (1,)), ((), ())), preferred_element_type=F32)


def gelu(x):
    half = 0.5 * x
    return half + half * lax.erf(x * 0.7071067811865476)


def slot(owner, owners, odd):
    return ((owner & 1) ^ odd) * (owners // 2) + owner // 2


def column_table(columns):
    turns = np.arange(columns)[:, None] * np.arange(MW)[None, :] % columns
    angle = turns * (2 * np.pi / columns)
    return np.concatenate([np.cos(angle), -np.sin(angle)], axis=1)


def row_table(height, strip_rows):
    freqs = np.arange(MH // 2 + 1)
    turns = freqs[None, :, None] * np.arange(height).reshape(-1, 1, strip_rows) % height
    angle = turns * (2 * np.pi / height)
    both = np.concatenate([np.cos(angle), np.sin(angle)], axis=1)
    return both.reshape(both.shape[0], 1, -1).astype(np.float32)


def pieces(kh, per_owner):
    count = min(MW, per_owner)
    for first in range(0, MW, count):
        mode = kh * MW + first
        yield mode // per_owner, mode % per_owner, first, count


def kv_kernel(me_ref, x_ref, w_ref, keep_ref, send_ref, w_t, acc):
    step = pl.program_id(0)
    channels = HEADS * HD

    @pl.when(step == 0)
    def _():
        w_t[...] = w_ref[...].T
        acc[...] = jnp.zeros_like(acc)

    total = acc[...]
    for at in range(0, x_ref.shape[0], SUB):
        x = x_ref[at : at + SUB, :]
        both = mm_nt(w_t[channels:, :], x)
        shaped = both.reshape(2 * HEADS, HD, SUB)
        center = shaped - jnp.sum(shaped, axis=1, keepdims=True) * (1.0 / HD)
        spread = jnp.sum(center * center, axis=1, keepdims=True) * (1.0 / HD) + EPSILON
        normed = (center * lax.rsqrt(spread)).reshape(2 * channels, SUB).astype(BF16)
        total = total + mm_nt(normed[:channels], normed[channels:])
    acc[...] = total

    @pl.when(step == pl.num_programs(0) - 1)
    def _():
        left = lax.broadcasted_iota(jnp.int32, (HD, 2 * HD), 1) < HD
        pairs = []
        for row in range(0, channels, 2 * HD):
            cols = slice(row, row + 2 * HD)
            pairs.append(jnp.where(left, total[row : row + HD, cols], total[row + HD : row + 2 * HD, cols]))
        odd = me_ref[0] == 1
        keep_ref[...] = jnp.where(odd, pairs[1], pairs[0])
        send_ref[...] = jnp.where(odd, pairs[0], pairs[1])


def field_kernel(cells, me_ref, x_ref, kva_ref, kvb_ref, wq_ref, wa_ref, wi_ref, wo_ref, tab_ref, ang_ref,
                 second_ref, keep_ref, send_ref, scaled, spectra, terms):
    step = pl.program_id(0)
    channels = HEADS * HD
    rows = spectra.shape[0]

    @pl.when(step == 0)
    def _():
        odd = me_ref[0] == 1
        mine, theirs = kva_ref[...] / cells, kvb_ref[...] / cells
        packed = (jnp.where(odd, theirs, mine), jnp.where(odd, mine, theirs))
        left = lax.broadcasted_iota(jnp.int32, (HD, 2 * HD), 1) < HD
        blank = jnp.zeros((HD, 2 * HD), F32)
        blocks = []
        for pair in range(HEADS // 2):
            part = packed[pair]
            for mine in (jnp.where(left, part, 0.0), jnp.where(left, 0.0, part)):
                line = [blank] * (HEADS // 2)
                line[pair] = mine
                blocks.append(jnp.concatenate(line, axis=1))
        scaled[...] = jnp.concatenate(blocks, axis=0).astype(BF16)

    for at in range(0, x_ref.shape[0], SUB):
        x = x_ref[at : at + SUB, :]
        queries = mm(x, wq_ref[...]).astype(BF16)
        attended = mm(queries, scaled[...]).astype(BF16)
        first = (x.astype(F32) + mm(attended, wa_ref[...])).astype(BF16)
        hidden = gelu(mm(first, wi_ref[...])).astype(BF16)
        second_ref[at : at + SUB, :] = (first.astype(F32) + mm(hidden, wo_ref[...])).astype(BF16)
    spectra[step] = mm(tab_ref[...], second_ref[...])

    @pl.when(step == pl.num_programs(0) - 1)
    def _():
        owners, per_owner, _ = terms.shape
        for f in range(MH // 2 + 1):
            parts = [jnp.zeros((MW, channels), F32)] * 4
            for r in range(rows):
                cos = ang_ref[0, 0, f * rows + r]
                sin = ang_ref[0, 0, (MH // 2 + 1 + f) * rows + r]
                re = spectra[r, :MW, :]
                im = spectra[r, MW:, :]
                parts = [parts[0] + cos * re, parts[1] + cos * im, parts[2] + sin * re, parts[3] + sin * im]
            cr, ci, sr, si = parts
            found = []
            if f < MH // 2:
                found.append((f, cr + si, ci - sr))
            if f > 0:
                found.append((MH - f, cr - si, ci + sr))
            for kh, re, im in found:
                for owner, row, kw, count in pieces(kh, per_owner):
                    at = slot(owner, owners, me_ref[0])
                    terms[at, row : row + count, :channels] = re[kw : kw + count]
                    terms[at, row : row + count, channels:] = im[kw : kw + count]
        keep_ref[...] = terms[: owners // 2]
        send_ref[...] = terms[owners // 2 :].astype(BF16)


def mode_kernel(terms_ref, w_ref, out_ref):
    step = pl.program_id(0)
    group = w_ref.shape[0]
    channels = HEADS * HD
    rows = pl.ds(pl.multiple_of(step * group, group), group)
    coeff = jnp.sum(terms_ref[:, rows, :].astype(F32), axis=0).astype(BF16).astype(F32)
    re, im = coeff[:, :channels], coeff[:, channels:]
    lhs = jnp.concatenate(
        [jnp.concatenate([re, -im], axis=1), jnp.concatenate([im, re], axis=1)], axis=0
    ).astype(BF16)
    index = lax.broadcasted_iota(jnp.int32, (2 * group, channels), 0) % group
    mixed = jnp.zeros((2 * group, channels), F32)
    for m in range(group):
        mixed = jnp.where(index == m, mm(lhs, w_ref[m]), mixed)
    for copy in range(out_ref.shape[0]):
        out_ref[copy, :, :channels] = mixed[:group].astype(BF16)
        out_ref[copy, :, channels:] = mixed[group:].astype(BF16)


def last_kernel(cells, me_ref, second_ref, lo_ref, hi_ref, ws_ref, tab_ref, ang_ref, out_ref, mixed, sums, diffs):
    step = pl.program_id(0)
    channels = HEADS * HD
    rows = pl.num_programs(0)
    half = MH // 2

    @pl.when(step == 0)
    def _():
        owners, per_owner, _ = mixed.shape
        mixed[: owners // 2] = lo_ref[...].astype(F32)
        mixed[owners // 2 :] = hi_ref[...].astype(F32)

        def read(kh):
            found = []
            for owner, row, _, count in pieces(kh, per_owner):
                at = slot(owner, owners, me_ref[0])
                found.append(mixed[at, row : row + count, :])
            return found[0] if len(found) == 1 else jnp.concatenate(found, axis=0)

        for f in range(half + 1):
            if f == 0:
                plus = read(0)
                sums[f] = plus
                diffs[f] = plus
            elif f == half:
                minus = read(half)
                sums[f] = minus
                diffs[f] = -minus
            else:
                plus, minus = read(f), read(MH - f)
                sums[f] = plus + minus
                diffs[f] = plus - minus

    re = jnp.zeros((MW, channels), F32)
    im = jnp.zeros((MW, channels), F32)
    for f in range(half + 1):
        cos = ang_ref[0, 0, f * rows + step]
        sin = ang_ref[0, 0, (half + 1 + f) * rows + step]
        re = re + cos * sums[f, :, :channels] - sin * diffs[f, :, channels:]
        im = im + cos * sums[f, :, channels:] + sin * diffs[f, :, :channels]
    kw = lax.broadcasted_iota(jnp.int32, (MW, channels), 0)
    weight = jnp.where(kw == 0, 1.0, 2.0) / cells
    back = jnp.concatenate([re * weight, im * weight], axis=0).astype(BF16)
    for at in range(0, second_ref.shape[0], SUB):
        here = slice(at, at + SUB)
        value = mm(second_ref[here, :], ws_ref[...]) + mm(tab_ref[here, :], back)
        out_ref[here, :] = gelu(value).astype(BF16)


def whole(shape):
    return pl.BlockSpec(shape, lambda *_: (0,) * len(shape))


def local(field, w_qkv, w_attn, w_inner, w_outer, w_skip, w_modes):
    strip_rows, columns, channels = field.shape
    hidden = w_inner.shape[1]
    size = lax.axis_size("row")
    bits = size.bit_length() - 1
    assert size == 1 << bits and size > 1
    me = lax.axis_index("row")
    height = strip_rows * size
    cells = float(height * columns)
    per_owner = w_modes.shape[0]
    ids = jnp.stack([me & 1, me]).astype(jnp.int32)
    chips = [list(range(core, size, 2)) for core in (0, 1)]

    def swap(value, distance):
        return lax.ppermute(value, "row", [(i, i ^ distance) for i in range(size)])

    table = column_table(columns)
    wide = jnp.asarray(table.T, BF16)
    tall = jnp.asarray(table, BF16)
    angles = jnp.asarray(row_table(height, strip_rows))
    per_row = pl.BlockSpec((None, columns, channels), lambda r, *_: (r, 0, 0))
    angle_spec = pl.BlockSpec((1, 1, angles.shape[2]), lambda r, ids_ref: (ids_ref[1], 0, 0), memory_space=pltpu.SMEM)

    kv_shape = (HD, 2 * HD)
    keep, send = pl.pallas_call(
        kv_kernel,
        out_shape=[jax.ShapeDtypeStruct(kv_shape, F32)] * 2,
        grid_spec=pltpu.PrefetchScalarGridSpec(
            num_scalar_prefetch=1,
            grid=(strip_rows,),
            in_specs=[per_row, whole(w_qkv.shape)],
            out_specs=[whole(kv_shape)] * 2,
            scratch_shapes=[pltpu.VMEM((3 * channels, channels), BF16), pltpu.VMEM((channels, channels), F32)],
        ),
        name="kv",
    )(ids, field, w_qkv)
    kv = keep + swap(send, 1)
    for b in range(1, bits - 2):
        kv = kv + swap(kv, 1 << b)
    kv = kv + swap(kv, size // 4) + swap(kv, size // 2) + swap(kv, 3 * size // 4)
    other = swap(kv, 1)

    half = (size // 2, per_owner, 2 * channels)
    second, keep, send = pl.pallas_call(
        functools.partial(field_kernel, cells),
        out_shape=[
            jax.ShapeDtypeStruct(field.shape, BF16),
            jax.ShapeDtypeStruct(half, F32),
            jax.ShapeDtypeStruct(half, BF16),
        ],
        grid_spec=pltpu.PrefetchScalarGridSpec(
            num_scalar_prefetch=1,
            grid=(strip_rows,),
            in_specs=[
                per_row,
                whole(kv_shape),
                whole(kv_shape),
                whole((channels, channels)),
                whole(w_attn.shape),
                whole(w_inner.shape),
                whole(w_outer.shape),
                whole(wide.shape),
                angle_spec,
            ],
            out_specs=[per_row, whole(half), whole(half)],
            scratch_shapes=[
                pltpu.VMEM((channels, channels), BF16),
                pltpu.VMEM((strip_rows, 2 * MW, channels), F32),
                pltpu.VMEM((size, per_owner, 2 * channels), F32),
            ],
        ),
        name="field",
    )(ids, field, kv, other, w_qkv, w_attn, w_inner, w_outer, wide, angles)

    both = (keep + swap(send, 1).astype(F32)).astype(BF16)
    terms = lax.all_to_all(both, "row", 0, 0, axis_index_groups=chips, tiled=True)

    group = 8
    copies = pl.pallas_call(
        mode_kernel,
        out_shape=jax.ShapeDtypeStruct(half, BF16),
        grid=(per_owner // group,),
        in_specs=[
            whole(half),
            pl.BlockSpec((group, 2 * channels, channels), lambda m: (m, 0, 0)),
        ],
        out_specs=pl.BlockSpec((size // 2, group, 2 * channels), lambda m: (0, m, 0)),
        name="modes",
    )(terms, w_modes.reshape(per_owner, 2 * channels, channels))

    held = lax.all_to_all(copies, "row", 0, 0, axis_index_groups=chips, tiled=True)
    far = swap(held, 1)

    return pl.pallas_call(
        functools.partial(last_kernel, cells),
        out_shape=jax.ShapeDtypeStruct(field.shape, BF16),
        grid_spec=pltpu.PrefetchScalarGridSpec(
            num_scalar_prefetch=1,
            grid=(strip_rows,),
            in_specs=[
                per_row,
                whole(half),
                whole(half),
                whole(w_skip.shape),
                whole(tall.shape),
                angle_spec,
            ],
            out_specs=per_row,
            scratch_shapes=[
                pltpu.VMEM((size, per_owner, 2 * channels), F32),
                pltpu.VMEM((MH // 2 + 1, MW, 2 * channels), F32),
                pltpu.VMEM((MH // 2 + 1, MW, 2 * channels), F32),
            ],
        ),
        name="last",
    )(ids, second, held, far, w_skip, tall, angles)


def solution(mesh):
    placed = (P(("grp", "row"), None, None), P(), P(), P(), P(), P(), P("row", None, None, None))
    return jax.shard_map(
        local, mesh=mesh, in_specs=placed, out_specs=P(("grp", "row"), None, None), check_vma=False
    )
```

```python
import functools

import jax
import jax.numpy as jnp
import numpy as np
from jax import lax
from jax.experimental import pallas as pl
from jax.experimental.pallas import tpu as pltpu
from jax.sharding import PartitionSpec as P

HEADS = 4
HD = 64
MH = 32
MW = 16
EPSILON = 1e-05
SUB = 256
F32 = jnp.float32
BF16 = jnp.bfloat16


def mm(a, b):
    return jnp.dot(a, b, preferred_element_type=F32)


def mm_nt(a, b):
    return lax.dot_general(a, b, (((1,), (1,)), ((), ())), preferred_element_type=F32)


def gelu(x):
    half = 0.5 * x
    return half + half * lax.erf(x * 0.7071067811865476)


def slot(owner, owners, odd):
    return ((owner & 1) ^ odd) * (owners // 2) + owner // 2


def skewed(stages, count):
    held = [None] * count
    for at in range(count + len(stages) - 1):
        for k in reversed(range(len(stages))):
            if 0 <= at - k < count:
                held[at - k] = stages[k](at - k, held[at - k])


def column_table(columns):
    turns = np.arange(columns)[:, None] * np.arange(MW)[None, :] % columns
    angle = turns * (2 * np.pi / columns)
    return np.concatenate([np.cos(angle), -np.sin(angle)], axis=1)


def row_table(height, strip_rows):
    freqs = np.arange(MH // 2 + 1)
    turns = freqs[None, :, None] * np.arange(height).reshape(-1, 1, strip_rows) % height
    angle = turns * (2 * np.pi / height)
    both = np.concatenate([np.cos(angle), np.sin(angle)], axis=1)
    return both.reshape(both.shape[0], 1, -1).astype(np.float32)


def pieces(kh, per_owner):
    count = min(MW, per_owner)
    for first in range(0, MW, count):
        mode = kh * MW + first
        yield mode // per_owner, mode % per_owner, first, count


def kv_kernel(me_ref, x_ref, w_ref, wa_ref, wi_ref, wo_ref, keep_ref, send_ref, wa_near, wi_near, wo_near,
              w_t, normed, acc, arrived):
    step = pl.program_id(0)
    channels = HEADS * HD
    fetches = [
        pltpu.make_async_copy(far, to, arrived.at[i])
        for i, (far, to) in enumerate(((wa_ref, wa_near), (wi_ref, wi_near), (wo_ref, wo_near)))
    ]

    @pl.when(step == 0)
    def _():
        for fetch in fetches:
            fetch.start()
        w_t[...] = w_ref[:, channels:].T
        normed[...] = jnp.zeros_like(normed)
        acc[...] = jnp.zeros_like(acc)

    acc[...] += mm_nt(normed[:channels, :], normed[channels:, :])

    def project(block, _):
        return mm_nt(w_t[...], x_ref[block * SUB : (block + 1) * SUB, :])

    def normalize(block, both):
        shaped = both.reshape(2 * HEADS, HD, SUB)
        center = shaped - jnp.sum(shaped, axis=1, keepdims=True) * (1.0 / HD)
        spread = jnp.sum(center * center, axis=1, keepdims=True) * (1.0 / HD) + EPSILON
        scaled = center * lax.rsqrt(spread)
        normed[:, block * SUB : (block + 1) * SUB] = scaled.reshape(2 * channels, SUB).astype(BF16)

    skewed([project, normalize], x_ref.shape[0] // SUB)

    @pl.when(step == pl.num_programs(0) - 1)
    def _():
        total = acc[...] + mm_nt(normed[:channels, :], normed[channels:, :])
        left = lax.broadcasted_iota(jnp.int32, (HD, 2 * HD), 1) < HD
        pairs = []
        for row in range(0, channels, 2 * HD):
            cols = slice(row, row + 2 * HD)
            pairs.append(jnp.where(left, total[row : row + HD, cols], total[row + HD : row + 2 * HD, cols]))
        odd = me_ref[0] == 1
        keep_ref[...] = jnp.where(odd, pairs[1], pairs[0])
        send_ref[...] = jnp.where(odd, pairs[0], pairs[1])
        for fetch in fetches:
            fetch.wait()


def field_kernel(cells, me_ref, x_ref, kva_ref, kvb_ref, wq_ref, wa_ref, wi_ref, wo_ref, tab_ref, ang_ref, far_ref,
                 second_ref, keep_ref, send_ref, near_ref, scaled, cosines, sines, terms, arrived):
    step = pl.program_id(0)
    channels = HEADS * HD
    rows = pl.num_programs(0)
    fetch = pltpu.make_async_copy(far_ref, near_ref, arrived)

    @pl.when(step == 0)
    def _():
        fetch.start()
        second_ref[0] = jnp.zeros(second_ref.shape[1:], BF16)
        cosines[...] = jnp.zeros_like(cosines)
        sines[...] = jnp.zeros_like(sines)
        odd = me_ref[0] == 1
        mine, theirs = kva_ref[...] / cells, kvb_ref[...] / cells
        packed = (jnp.where(odd, theirs, mine), jnp.where(odd, mine, theirs))
        left = lax.broadcasted_iota(jnp.int32, (HD, 2 * HD), 1) < HD
        blank = jnp.zeros((HD, 2 * HD), F32)
        blocks = []
        for pair in range(HEADS // 2):
            part = packed[pair]
            for mine in (jnp.where(left, part, 0.0), jnp.where(left, 0.0, part)):
                line = [blank] * (HEADS // 2)
                line[pair] = mine
                blocks.append(jnp.concatenate(line, axis=1))
        scaled[...] = jnp.concatenate(blocks, axis=0).astype(BF16)

    columns = x_ref.shape[1]
    per_row = columns // SUB

    def place(block):
        return step, slice(block * SUB, (block + 1) * SUB)

    def ask(block, _):
        row, here = place(block)
        return mm(x_ref[row, here, :], wq_ref[...]).astype(BF16)

    def attend(block, queries):
        return mm(queries, scaled[...]).astype(BF16)

    def add(block, attended):
        row, here = place(block)
        return (x_ref[row, here, :].astype(F32) + mm(attended, wa_ref[...])).astype(BF16)

    def widen(block, first):
        return first, gelu(mm(first, wi_ref[...])).astype(BF16)

    def narrow(block, pair):
        row, here = place(block)
        first, hidden = pair
        second_ref[row, here, :] = (first.astype(F32) + mm(hidden, wo_ref[...])).astype(BF16)

    def transform(row):
        spectrum = mm(tab_ref[...], second_ref[row])
        for f in range(MH // 2 + 1):
            cosines[f] += ang_ref[0, 0, f * rows + row] * spectrum
            sines[f] += ang_ref[0, 0, (MH // 2 + 1 + f) * rows + row] * spectrum

    transform(jnp.maximum(step - 1, 0))
    skewed([ask, attend, add, widen, narrow], per_row)

    @pl.when(step == pl.num_programs(0) - 1)
    def _():
        transform(step)
        owners, per_owner, _ = terms.shape
        for f in range(MH // 2 + 1):
            cr, ci = cosines[f, :MW, :], cosines[f, MW:, :]
            sr, si = sines[f, :MW, :], sines[f, MW:, :]
            found = []
            if f < MH // 2:
                found.append((f, cr + si, ci - sr))
            if f > 0:
                found.append((MH - f, cr - si, ci + sr))
            for kh, re, im in found:
                for owner, row, kw, count in pieces(kh, per_owner):
                    at = slot(owner, owners, me_ref[0])
                    terms[at, row : row + count, :channels] = re[kw : kw + count]
                    terms[at, row : row + count, channels:] = im[kw : kw + count]
        fetch.wait()
        keep_ref[...] = terms[: owners // 2]
        send_ref[...] = terms[owners // 2 :].astype(BF16)


def mode_kernel(terms_ref, w_ref, out_ref):
    step = pl.program_id(0)
    group = out_ref.shape[1]
    channels = HEADS * HD
    rows = pl.ds(pl.multiple_of(step * group, group), group)
    coeff = jnp.sum(terms_ref[:, rows, :].astype(F32), axis=0).astype(BF16).astype(F32)
    re, im = coeff[:, :channels], coeff[:, channels:]
    lhs = jnp.concatenate(
        [jnp.concatenate([re, -im], axis=1), jnp.concatenate([im, re], axis=1)], axis=0
    ).astype(BF16)
    index = lax.broadcasted_iota(jnp.int32, (2 * group, channels), 0) % group
    mixed = jnp.zeros((2 * group, channels), F32)
    for m in range(group):
        mixed = jnp.where(index == m, mm(lhs, w_ref[step * group + m]), mixed)
    for copy in range(out_ref.shape[0]):
        out_ref[copy, :, :channels] = mixed[:group].astype(BF16)
        out_ref[copy, :, channels:] = mixed[group:].astype(BF16)


def last_kernel(cells, me_ref, second_ref, lo_ref, hi_ref, ws_ref, tab_ref, ang_ref, out_ref, mixed, sums, diffs, back):
    step = pl.program_id(0)
    channels = HEADS * HD
    rows = pl.num_programs(0)
    half = MH // 2

    def turn(row):
        re = jnp.zeros((MW, channels), F32)
        im = jnp.zeros((MW, channels), F32)
        for f in range(half + 1):
            cos = ang_ref[0, 0, f * rows + row]
            sin = ang_ref[0, 0, (half + 1 + f) * rows + row]
            re = re + cos * sums[f, :, :channels] - sin * diffs[f, :, channels:]
            im = im + cos * sums[f, :, channels:] + sin * diffs[f, :, :channels]
        kw = lax.broadcasted_iota(jnp.int32, (MW, channels), 0)
        weight = jnp.where(kw == 0, 1.0, 2.0) / cells
        back[row % 2] = jnp.concatenate([re * weight, im * weight], axis=0).astype(BF16)

    @pl.when(step == 0)
    def _():
        owners, per_owner, _ = mixed.shape
        mixed[: owners // 2] = lo_ref[...].astype(F32)
        mixed[owners // 2 :] = hi_ref[...].astype(F32)

        def read(kh):
            found = []
            for owner, row, _, count in pieces(kh, per_owner):
                at = slot(owner, owners, me_ref[0])
                found.append(mixed[at, row : row + count, :])
            return found[0] if len(found) == 1 else jnp.concatenate(found, axis=0)

        for f in range(half + 1):
            if f == 0:
                plus = read(0)
                sums[f] = plus
                diffs[f] = plus
            elif f == half:
                minus = read(half)
                sums[f] = minus
                diffs[f] = -minus
            else:
                plus, minus = read(f), read(MH - f)
                sums[f] = plus + minus
                diffs[f] = plus - minus

        turn(0)

    def skip(block, _):
        return mm(second_ref[step, block * SUB : (block + 1) * SUB, :], ws_ref[...])

    def spread(block, value):
        return value + mm(tab_ref[block * SUB : (block + 1) * SUB, :], back[step % 2])

    def finish(block, value):
        out_ref[block * SUB : (block + 1) * SUB, :] = gelu(value).astype(BF16)

    skewed([skip, spread, finish], second_ref.shape[1] // SUB)
    turn(jnp.minimum(step + 1, rows - 1))


def whole(shape):
    return pl.BlockSpec(shape, lambda *_: (0,) * len(shape))


def near(value):
    return pltpu.with_memory_space_constraint(value, pltpu.VMEM)


def away(value):
    return pltpu.with_memory_space_constraint(value, pltpu.HBM)


HERE = pl.BlockSpec(memory_space=pltpu.VMEM)


def local(field, w_qkv, w_attn, w_inner, w_outer, w_skip, w_modes):
    strip_rows, columns, channels = field.shape
    hidden = w_inner.shape[1]
    size = lax.axis_size("row")
    bits = size.bit_length() - 1
    assert size == 1 << bits and size > 1
    me = lax.axis_index("row")
    height = strip_rows * size
    cells = float(height * columns)
    per_owner = w_modes.shape[0]
    ids = jnp.stack([me & 1, me]).astype(jnp.int32)
    chips = [list(range(core, size, 2)) for core in (0, 1)]

    def swap(value, distance):
        return lax.ppermute(value, "row", [(i, i ^ distance) for i in range(size)])

    table = column_table(columns)
    wide = jnp.asarray(table.T, BF16)
    tall = jnp.asarray(table, BF16)
    angles = jnp.asarray(row_table(height, strip_rows))
    per_row = pl.BlockSpec((None, columns, channels), lambda r, *_: (r, 0, 0))
    angle_spec = pl.BlockSpec((1, 1, angles.shape[2]), lambda r, ids_ref: (ids_ref[1], 0, 0), memory_space=pltpu.SMEM)

    kv_shape = (HD, 2 * HD)
    hbm = pl.BlockSpec(memory_space=pltpu.HBM)
    keep, send, wa_near, wi_near, wo_near = pl.pallas_call(
        kv_kernel,
        out_shape=[pltpu.VMEM(kv_shape, F32)] * 2 + [pltpu.VMEM(w.shape, BF16) for w in (w_attn, w_inner, w_outer)],
        grid_spec=pltpu.PrefetchScalarGridSpec(
            num_scalar_prefetch=1,
            grid=(strip_rows,),
            in_specs=[per_row, whole(w_qkv.shape), hbm, hbm, hbm],
            out_specs=[HERE] * 5,
            scratch_shapes=[
                pltpu.VMEM((2 * channels, channels), BF16),
                pltpu.VMEM((2 * channels, columns), BF16),
                pltpu.VMEM((channels, channels), F32),
                pltpu.SemaphoreType.DMA((3,)),
            ],
        ),
        compiler_params=pltpu.CompilerParams(vmem_limit_bytes=12 << 20),
        name="kv",
    )(ids, away(field), away(w_qkv), away(w_attn), away(w_inner), away(w_outer))
    kv = keep + swap(send, 1)
    for b in range(1, bits, 2):
        steps = [1 << b] if b + 1 == bits else [1 << b, 2 << b, 3 << b]
        kv = sum((swap(kv, d) for d in steps), kv)
    other = swap(kv, 1)

    half = (size // 2, per_owner, 2 * channels)
    mode_shape = (per_owner, 2 * channels, channels)
    second, keep, send, w_near = pl.pallas_call(
        functools.partial(field_kernel, cells),
        out_shape=[
            pltpu.VMEM(field.shape, BF16),
            pltpu.VMEM(half, F32),
            pltpu.VMEM(half, BF16),
            pltpu.VMEM(mode_shape, BF16),
        ],
        grid_spec=pltpu.PrefetchScalarGridSpec(
            num_scalar_prefetch=1,
            grid=(strip_rows,),
            in_specs=[
                HERE,
                whole(kv_shape),
                whole(kv_shape),
                whole((channels, channels)),
                whole(w_attn.shape),
                whole(w_inner.shape),
                whole(w_outer.shape),
                whole(wide.shape),
                angle_spec,
                hbm,
            ],
            out_specs=[HERE, HERE, HERE, HERE],
            scratch_shapes=[
                pltpu.VMEM((channels, channels), BF16),
                pltpu.VMEM((MH // 2 + 1, 2 * MW, channels), F32),
                pltpu.VMEM((MH // 2 + 1, 2 * MW, channels), F32),
                pltpu.VMEM((size, per_owner, 2 * channels), F32),
                pltpu.SemaphoreType.DMA(()),
            ],
        ),
        compiler_params=pltpu.CompilerParams(vmem_limit_bytes=14 << 20),
        name="field",
    )(ids, near(field), kv, other, near(w_qkv), near(wa_near), near(wi_near), near(wo_near), near(wide), angles, away(w_modes.reshape(mode_shape)))

    both = (keep + swap(send, 1).astype(F32)).astype(BF16)
    terms = lax.all_to_all(both, "row", 0, 0, axis_index_groups=chips, tiled=True)

    group = 8
    copies = pl.pallas_call(
        mode_kernel,
        out_shape=jax.ShapeDtypeStruct(half, BF16),
        grid=(per_owner // group,),
        in_specs=[
            whole(half),
            HERE,
        ],
        out_specs=pl.BlockSpec((size // 2, group, 2 * channels), lambda m: (0, m, 0)),
        compiler_params=pltpu.CompilerParams(vmem_limit_bytes=4 << 20),
        name="modes",
    )(terms, near(w_near))

    held = lax.all_to_all(copies, "row", 0, 0, axis_index_groups=chips, tiled=True)
    far = swap(held, 1)

    return pl.pallas_call(
        functools.partial(last_kernel, cells),
        out_shape=jax.ShapeDtypeStruct(field.shape, BF16),
        grid_spec=pltpu.PrefetchScalarGridSpec(
            num_scalar_prefetch=1,
            grid=(strip_rows,),
            in_specs=[
                HERE,
                whole(half),
                whole(half),
                whole(w_skip.shape),
                whole(tall.shape),
                angle_spec,
            ],
            out_specs=per_row,
            scratch_shapes=[
                pltpu.VMEM((size, per_owner, 2 * channels), F32),
                pltpu.VMEM((MH // 2 + 1, MW, 2 * channels), F32),
                pltpu.VMEM((MH // 2 + 1, MW, 2 * channels), F32),
                pltpu.VMEM((2, 2 * MW, channels), BF16),
            ],
        ),
        compiler_params=pltpu.CompilerParams(vmem_limit_bytes=12 << 20),
        name="last",
    )(ids, near(second), held, far, w_skip, tall, angles)


def solution(mesh):
    placed = (P(("grp", "row"), None, None), P(), P(), P(), P(), P(), P("row", None, None, None))
    return jax.shard_map(
        local, mesh=mesh, in_specs=placed, out_specs=P(("grp", "row"), None, None), check_vma=False
    )
```

```python
import functools

import jax
import jax.numpy as jnp
import numpy as np
from jax import lax
from jax.experimental import pallas as pl
from jax.experimental.pallas import tpu as pltpu
from jax.sharding import PartitionSpec as P

HEADS = 4
HD = 64
MH = 32
MW = 16
EPSILON = 1e-05
SUB = 512
KV_SUB = 256
F32 = jnp.float32
BF16 = jnp.bfloat16


def mm(a, b):
    return jnp.dot(a, b, preferred_element_type=F32)


def mm_nt(a, b):
    return lax.dot_general(a, b, (((1,), (1,)), ((), ())), preferred_element_type=F32)


def gelu(x):
    half = 0.5 * x
    return half + half * lax.erf(x * 0.7071067811865476)


def skewed(stages, count):
    held = [None] * count
    for at in range(count + len(stages) - 1):
        for k in reversed(range(len(stages))):
            if 0 <= at - k < count:
                held[at - k] = stages[k](at - k, held[at - k])


def column_table(columns):
    turns = np.arange(columns)[:, None] * np.arange(MW)[None, :] % columns
    angle = turns * (2 * np.pi / columns)
    return np.concatenate([np.cos(angle), -np.sin(angle)], axis=1)


def split(ref, at, value):
    for block in range(value.shape[1] // 128):
        ref[block, at, :] = value[:, block * 128 : (block + 1) * 128]


def join(ref, at, blocks):
    return jnp.concatenate([ref[block, at, :] for block in blocks], axis=1)


def halves(value):
    high = value.astype(BF16)
    return high, (value - np.asarray(high, np.float64)).astype(BF16)


def placing(size, per_owner, odd):
    if per_owner < MW:
        return list(range(MH))
    group = per_owner // MW
    owners = [*range(odd, size, 2), *range(1 - odd, size, 2)]
    return [owner * group + k for owner in owners for k in range(group)]


def rows_of(kw, per_owner, odd):
    if per_owner >= MW:
        return pl.ds(kw, MH, stride=MW)
    part = kw // per_owner
    first = ((part & 1) ^ odd) * (MH * MW // 2) + part // 2 * per_owner + kw % per_owner
    return pl.ds(first, MH, stride=MW // 2)


def row_tables(size, strip_rows, per_owner):
    height = size * strip_rows
    ahead, back = [], []
    for me in range(size):
        order = np.array(placing(size, per_owner, me & 1))
        freqs = np.where(order < MH // 2, order, order - MH + height)
        angle = freqs[:, None] * (me * strip_rows + np.arange(strip_rows))[None, :] % height * (2 * np.pi / height)
        cos, sin = np.cos(angle), np.sin(angle)
        real = np.stack([cos, sin], axis=2).reshape(MH, -1)
        imag = np.stack([-sin, cos], axis=2).reshape(MH, -1)
        high, low = halves(np.concatenate([real, imag]))
        ahead.append(np.concatenate([high, high, low], axis=1))
        real = np.concatenate([cos, -sin]).T
        imag = np.concatenate([sin, cos]).T
        back.append(np.concatenate(halves(np.stack([real, imag], axis=1).reshape(2 * strip_rows, -1)), axis=1))
    return np.stack(ahead), np.stack(back)


def kv_kernel(me_ref, far_ref, w_ref, wa_ref, wi_ref, wo_ref, keep_ref, send_ref, x_ref, wa_near, wi_near, wo_near,
              w_t, normed, acc, arrived, landed):
    step = pl.program_id(0)
    channels = HEADS * HD
    fetches = [
        pltpu.make_async_copy(far, to, arrived.at[i])
        for i, (far, to) in enumerate(((wa_ref, wa_near), (wi_ref, wi_near), (wo_ref, wo_near)))
    ]

    def row_copy(row):
        return pltpu.make_async_copy(far_ref.at[row], x_ref.at[row], landed.at[row])

    @pl.when(step == 0)
    def _():
        for row in range(x_ref.shape[0]):
            row_copy(row).start()
        for fetch in fetches:
            fetch.start()
        w_t[...] = w_ref[:, channels:].T
        normed[...] = jnp.zeros_like(normed)
        acc[...] = jnp.zeros_like(acc)

    row_copy(step).wait()
    acc[...] += mm_nt(normed[:channels, :], normed[channels:, :])

    def project(block, _):
        return mm_nt(w_t[...], x_ref[step, block * KV_SUB : (block + 1) * KV_SUB, :])

    def normalize(block, both):
        shaped = both.reshape(2 * HEADS, HD, KV_SUB)
        center = shaped - jnp.sum(shaped, axis=1, keepdims=True) * (1.0 / HD)
        spread = jnp.sum(center * center, axis=1, keepdims=True) * (1.0 / HD) + EPSILON
        scaled = center * lax.rsqrt(spread)
        normed[:, block * KV_SUB : (block + 1) * KV_SUB] = scaled.reshape(2 * channels, KV_SUB).astype(BF16)

    skewed([project, normalize], x_ref.shape[1] // KV_SUB)

    @pl.when(step == pl.num_programs(0) - 1)
    def _():
        total = acc[...] + mm_nt(normed[:channels, :], normed[channels:, :])
        left = lax.broadcasted_iota(jnp.int32, (HD, 2 * HD), 1) < HD
        pairs = []
        for row in range(0, channels, 2 * HD):
            cols = slice(row, row + 2 * HD)
            pairs.append(jnp.where(left, total[row : row + HD, cols], total[row + HD : row + 2 * HD, cols]))
        odd = me_ref[0] == 1
        keep_ref[...] = jnp.where(odd, pairs[1], pairs[0])
        send_ref[...] = jnp.where(odd, pairs[0], pairs[1])
        for fetch in fetches:
            fetch.wait()


def field_kernel(cells, me_ref, x_ref, kva_ref, kvb_ref, wq_ref, wa_ref, wi_ref, wo_ref, tab_ref, ang_ref, far_ref,
                 second_ref, keep_ref, send_ref, near_ref, scaled, spectra, terms, arrived):
    step = pl.program_id(0)
    channels = HEADS * HD
    rows = x_ref.shape[0]
    fetch = pltpu.make_async_copy(far_ref, near_ref, arrived)

    @pl.when(step == 0)
    def _():
        fetch.start()
        odd = me_ref[0] == 1
        mine, theirs = kva_ref[...] / cells, kvb_ref[...] / cells
        packed = (jnp.where(odd, theirs, mine), jnp.where(odd, mine, theirs))
        left = lax.broadcasted_iota(jnp.int32, (HD, 2 * HD), 1) < HD
        blank = jnp.zeros((HD, 2 * HD), F32)
        blocks = []
        for pair in range(HEADS // 2):
            part = packed[pair]
            for mine in (jnp.where(left, part, 0.0), jnp.where(left, 0.0, part)):
                line = [blank] * (HEADS // 2)
                line[pair] = mine
                blocks.append(jnp.concatenate(line, axis=1))
        scaled[...] = jnp.concatenate(blocks, axis=0).astype(BF16)

    columns = x_ref.shape[1]
    per_row = columns // SUB

    def place(block):
        return step, slice(block * SUB, (block + 1) * SUB)

    def ask(block, _):
        row, here = place(block)
        return mm(x_ref[row, here, :], wq_ref[...]).astype(BF16)

    def attend(block, queries):
        return mm(queries, scaled[...]).astype(BF16)

    def add(block, attended):
        row, here = place(block)
        return (x_ref[row, here, :].astype(F32) + mm(attended, wa_ref[...])).astype(BF16)

    def widen(block, first):
        return first, gelu(mm(first, wi_ref[...])).astype(BF16)

    def narrow(block, pair):
        row, here = place(block)
        first, hidden = pair
        second_ref[row, here, :] = (first.astype(F32) + mm(hidden, wo_ref[...])).astype(BF16)

    def transform(row):
        at = pl.ds(pl.multiple_of(row * 2 * MW, 2 * MW), 2 * MW)
        split(spectra, at, mm(tab_ref[...], second_ref[row]))

    skewed([ask, attend, add, widen, narrow], per_row)
    transform(step)

    @pl.when(step == pl.num_programs(0) - 1)
    def _():
        per_owner = keep_ref.shape[1]
        for kw in range(MW):
            spectrum = join(spectra, pl.ds(kw, 2 * rows, stride=MW), range(spectra.shape[0]))
            high = spectrum.astype(BF16)
            low = (spectrum - high.astype(F32)).astype(BF16)
            found = mm(ang_ref[...], jnp.concatenate([high, low, high], axis=0))
            at = rows_of(kw, per_owner, me_ref[0])
            split(terms, at, jnp.concatenate([found[:MH], found[MH:]], axis=1))
        fetch.wait()
        middle = MH * MW // 2
        for block in range(terms.shape[0]):
            here = slice(block * 128, (block + 1) * 128)
            keep_ref[:, :, here] = terms[block, :middle].reshape(keep_ref.shape[:2] + (128,))
            send_ref[:, :, here] = terms[block, middle:].astype(BF16).reshape(keep_ref.shape[:2] + (128,))


def mode_kernel(terms_ref, w_ref, out_ref):
    step = pl.program_id(0)
    group = out_ref.shape[1]
    channels = HEADS * HD
    rows = pl.ds(pl.multiple_of(step * group, group), group)
    coeff = jnp.sum(terms_ref[:, rows, :].astype(F32), axis=0).astype(BF16).astype(F32)
    re, im = coeff[:, :channels], coeff[:, channels:]
    lhs = jnp.concatenate(
        [jnp.concatenate([re, -im], axis=1), jnp.concatenate([im, re], axis=1)], axis=0
    ).astype(BF16)
    index = lax.broadcasted_iota(jnp.int32, (2 * group, channels), 0) % group
    mixed = jnp.zeros((2 * group, channels), F32)
    for m in range(group):
        mixed = jnp.where(index == m, mm(lhs, w_ref[step * group + m]), mixed)
    for copy in range(out_ref.shape[0]):
        out_ref[copy, :, :channels] = mixed[:group].astype(BF16)
        out_ref[copy, :, channels:] = mixed[group:].astype(BF16)


def last_kernel(cells, me_ref, second_ref, lo_ref, hi_ref, ws_ref, tab_ref, ang_ref, out_ref, mixed, back, held, sent):
    step = pl.program_id(0)
    channels = HEADS * HD
    rows = second_ref.shape[0]

    @pl.when(step == 0)
    def _():
        per_owner = lo_ref.shape[1]
        middle = MH * MW // 2
        split(mixed, slice(0, middle), lo_ref[...].astype(F32).reshape(middle, 2 * channels))
        split(mixed, slice(middle, None), hi_ref[...].astype(F32).reshape(middle, 2 * channels))
        for kw in range(MW):
            at = rows_of(kw, per_owner, me_ref[0])
            blocks = range(mixed.shape[0])
            re, im = join(mixed, at, blocks[: len(blocks) // 2]), join(mixed, at, blocks[len(blocks) // 2 :])
            both = jnp.concatenate([re, im], axis=0).astype(BF16)
            found = mm(ang_ref[...], jnp.concatenate([both, both], axis=0))
            split(back, pl.ds(kw, 2 * rows, stride=MW), found * ((2.0 if kw else 1.0) / cells))

    there = pl.ds(pl.multiple_of(step * 2 * MW, 2 * MW), 2 * MW)
    rhs = jnp.concatenate([ws_ref[...], join(back, there, range(back.shape[0])).astype(BF16)], axis=0)

    def both(block, _):
        here = slice(block * SUB, (block + 1) * SUB)
        return mm(jnp.concatenate([second_ref[step, here, :], tab_ref[here, :]], axis=1), rhs)

    blocks = second_ref.shape[1] // SUB

    def send(row, block):
        here = pl.ds(block * SUB, SUB)
        return pltpu.make_async_copy(held.at[row, here], out_ref.at[row, here], sent.at[row, block])

    def finish(block, value):
        held[step, block * SUB : (block + 1) * SUB, :] = gelu(value).astype(BF16)
        send(step, block).start()

    skewed([both, finish], blocks)

    @pl.when(step == pl.num_programs(0) - 1)
    def _():
        for row in range(rows):
            for block in range(blocks):
                send(row, block).wait()


def whole(shape):
    return pl.BlockSpec(shape, lambda *_: (0,) * len(shape))


def near(value):
    return pltpu.with_memory_space_constraint(value, pltpu.VMEM)


def away(value):
    return pltpu.with_memory_space_constraint(value, pltpu.HBM)


HERE = pl.BlockSpec(memory_space=pltpu.VMEM)


def local(field, w_qkv, w_attn, w_inner, w_outer, w_skip, w_modes):
    strip_rows, columns, channels = field.shape
    hidden = w_inner.shape[1]
    size = lax.axis_size("row")
    bits = size.bit_length() - 1
    assert size == 1 << bits and size > 1
    me = lax.axis_index("row")
    height = strip_rows * size
    cells = float(height * columns)
    per_owner = w_modes.shape[0]
    ids = jnp.stack([me & 1, me]).astype(jnp.int32)
    chips = [list(range(core, size, 2)) for core in (0, 1)]

    def swap(value, distance):
        return lax.ppermute(value, "row", [(i, i ^ distance) for i in range(size)])

    table = column_table(columns)
    wide = jnp.asarray(table.T, BF16)
    tall = jnp.asarray(table, BF16)
    ahead, behind = (jnp.asarray(t) for t in row_tables(size, strip_rows, per_owner))
    per_row = pl.BlockSpec((None, columns, channels), lambda r, *_: (r, 0, 0))

    def mine(tables):
        return pl.BlockSpec((None,) + tables.shape[1:], lambda r, ids_ref: (ids_ref[1], 0, 0))

    kv_shape = (HD, 2 * HD)
    hbm = pl.BlockSpec(memory_space=pltpu.HBM)
    keep, send, x_near, wa_near, wi_near, wo_near = pl.pallas_call(
        kv_kernel,
        out_shape=[pltpu.VMEM(kv_shape, F32)] * 2 + [pltpu.VMEM(w.shape, BF16) for w in (field, w_attn, w_inner, w_outer)],
        grid_spec=pltpu.PrefetchScalarGridSpec(
            num_scalar_prefetch=1,
            grid=(strip_rows,),
            in_specs=[hbm, whole(w_qkv.shape), hbm, hbm, hbm],
            out_specs=[HERE] * 6,
            scratch_shapes=[
                pltpu.VMEM((2 * channels, channels), BF16),
                pltpu.VMEM((2 * channels, columns), BF16),
                pltpu.VMEM((channels, channels), F32),
                pltpu.SemaphoreType.DMA((3,)),
                pltpu.SemaphoreType.DMA((strip_rows,)),
            ],
        ),
        compiler_params=pltpu.CompilerParams(vmem_limit_bytes=12 << 20),
        name="kv",
    )(ids, away(field), away(w_qkv), away(w_attn), away(w_inner), away(w_outer))
    kv = keep + swap(send, 1)
    for b in range(1, bits, 2):
        steps = [1 << b] if b + 1 == bits else [1 << b, 2 << b, 3 << b]
        kv = sum((swap(kv, d) for d in steps), kv)
    other = swap(kv, 1)

    half = (size // 2, per_owner, 2 * channels)
    mode_shape = (per_owner, 2 * channels, channels)
    second, keep, send, w_near = pl.pallas_call(
        functools.partial(field_kernel, cells),
        out_shape=[
            pltpu.VMEM(field.shape, BF16),
            pltpu.VMEM(half, F32),
            pltpu.VMEM(half, BF16),
            pltpu.VMEM(mode_shape, BF16),
        ],
        grid_spec=pltpu.PrefetchScalarGridSpec(
            num_scalar_prefetch=1,
            grid=(strip_rows,),
            in_specs=[
                HERE,
                whole(kv_shape),
                whole(kv_shape),
                whole((channels, channels)),
                whole(w_attn.shape),
                whole(w_inner.shape),
                whole(w_outer.shape),
                whole(wide.shape),
                mine(ahead),
                hbm,
            ],
            out_specs=[HERE, HERE, HERE, HERE],
            scratch_shapes=[
                pltpu.VMEM((channels, channels), BF16),
                pltpu.VMEM((channels // 128, strip_rows * 2 * MW, 128), F32),
                pltpu.VMEM((channels // 64, MH * MW, 128), F32),
                pltpu.SemaphoreType.DMA(()),
            ],
        ),
        compiler_params=pltpu.CompilerParams(vmem_limit_bytes=14 << 20),
        name="field",
    )(ids, near(x_near), kv, other, near(w_qkv), near(wa_near), near(wi_near), near(wo_near), near(wide), ahead, away(w_modes.reshape(mode_shape)))

    both = (keep + swap(send, 1).astype(F32)).astype(BF16)
    terms = lax.all_to_all(both, "row", 0, 0, axis_index_groups=chips, tiled=True)

    group = 8
    copies = pl.pallas_call(
        mode_kernel,
        out_shape=jax.ShapeDtypeStruct(half, BF16),
        grid=(per_owner // group,),
        in_specs=[
            whole(half),
            HERE,
        ],
        out_specs=pl.BlockSpec((size // 2, group, 2 * channels), lambda m: (0, m, 0)),
        compiler_params=pltpu.CompilerParams(vmem_limit_bytes=4 << 20),
        name="modes",
    )(terms, near(w_near))

    held = lax.all_to_all(copies, "row", 0, 0, axis_index_groups=chips, tiled=True)
    far = swap(held, 1)

    return pl.pallas_call(
        functools.partial(last_kernel, cells),
        out_shape=jax.ShapeDtypeStruct(field.shape, BF16),
        grid_spec=pltpu.PrefetchScalarGridSpec(
            num_scalar_prefetch=1,
            grid=(strip_rows,),
            in_specs=[
                HERE,
                whole(half),
                whole(half),
                whole(w_skip.shape),
                whole(tall.shape),
                mine(behind),
            ],
            out_specs=hbm,
            scratch_shapes=[
                pltpu.VMEM((channels // 64, MH * MW, 128), F32),
                pltpu.VMEM((channels // 128, strip_rows * 2 * MW, 128), F32),
                pltpu.VMEM(field.shape, BF16),
                pltpu.SemaphoreType.DMA((strip_rows, columns // SUB)),
            ],
        ),
        compiler_params=pltpu.CompilerParams(vmem_limit_bytes=12 << 20),
        name="last",
    )(ids, near(second), held, far, w_skip, tall, behind)


def solution(mesh):
    placed = (P(("grp", "row"), None, None), P(), P(), P(), P(), P(), P("row", None, None, None))
    return jax.shard_map(
        local, mesh=mesh, in_specs=placed, out_specs=P(("grp", "row"), None, None), check_vma=False
    )
```

```python
import functools

import jax
import jax.numpy as jnp
import numpy as np
from jax import lax
from jax.experimental import pallas as pl
from jax.experimental.pallas import tpu as pltpu
from jax.sharding import PartitionSpec as P

HEADS = 4
HD = 64
MH = 32
MW = 16
EPSILON = 1e-05
SUB = 512
KV_SUB = 256
LAST_SUB = 1024
ROWS = 2
F32 = jnp.float32
BF16 = jnp.bfloat16


def mm(a, b):
    return jnp.dot(a, b, preferred_element_type=F32)


def mm_nt(a, b):
    return lax.dot_general(a, b, (((1,), (1,)), ((), ())), preferred_element_type=F32)


def gelu(x):
    half = 0.5 * x
    return half + half * lax.erf(x * 0.7071067811865476)


def skewed(stages, count):
    held = [None] * count
    for at in range(count + len(stages) - 1):
        for k in reversed(range(len(stages))):
            if 0 <= at - k < count:
                held[at - k] = stages[k](at - k, held[at - k])


def column_table(columns):
    turns = np.arange(columns)[:, None] * np.arange(MW)[None, :] % columns
    angle = turns * (2 * np.pi / columns)
    return np.concatenate([np.cos(angle), -np.sin(angle)], axis=1)


def split(ref, at, value):
    for block in range(value.shape[1] // 128):
        ref[block, at, :] = value[:, block * 128 : (block + 1) * 128]


def join(ref, at, blocks):
    return jnp.concatenate([ref[block, at, :] for block in blocks], axis=1)


def halves(value):
    high = value.astype(BF16)
    return high, (value - np.asarray(high, np.float64)).astype(BF16)


def placing(size, per_owner, odd):
    if per_owner < MW:
        return list(range(MH))
    group = per_owner // MW
    owners = [*range(odd, size, 2), *range(1 - odd, size, 2)]
    return [owner * group + k for owner in owners for k in range(group)]


def rows_of(kw, per_owner, odd):
    if per_owner >= MW:
        return pl.ds(kw, MH, stride=MW)
    part = kw // per_owner
    first = ((part & 1) ^ odd) * (MH * MW // 2) + part // 2 * per_owner + kw % per_owner
    return pl.ds(first, MH, stride=MW // 2)


def row_tables(size, strip_rows, per_owner):
    height = size * strip_rows
    ahead, back = [], []
    for me in range(size):
        order = np.array(placing(size, per_owner, me & 1))
        freqs = np.where(order < MH // 2, order, order - MH + height)
        angle = freqs[:, None] * (me * strip_rows + np.arange(strip_rows))[None, :] % height * (2 * np.pi / height)
        cos, sin = np.cos(angle), np.sin(angle)
        real = np.stack([cos, sin], axis=2).reshape(MH, -1)
        imag = np.stack([-sin, cos], axis=2).reshape(MH, -1)
        high, low = halves(np.concatenate([real, imag]))
        ahead.append(np.concatenate([high, high, low], axis=1))
        real = np.concatenate([cos, -sin]).T
        imag = np.concatenate([sin, cos]).T
        back.append(np.concatenate(halves(np.stack([real, imag], axis=1).reshape(2 * strip_rows, -1)), axis=1))
    return np.stack(ahead), np.stack(back)


def kv_kernel(me_ref, far_ref, w_far, wa_ref, wi_ref, wo_ref, keep_ref, send_ref, x_ref, w_ref, wa_near, wi_near, wo_near,
              w_t, normed, acc, arrived, landed):
    step = pl.program_id(0)
    channels = HEADS * HD
    fetches = [
        pltpu.make_async_copy(far, to, arrived.at[i])
        for i, (far, to) in enumerate(((wa_ref, wa_near), (wi_ref, wi_near), (wo_ref, wo_near)))
    ]

    def row_copy(row):
        return pltpu.make_async_copy(far_ref.at[row], x_ref.at[row], landed.at[row])

    @pl.when(step == 0)
    def _():
        weights = pltpu.make_async_copy(w_far, w_ref, arrived.at[3])
        weights.start()
        for row in range(x_ref.shape[0]):
            row_copy(row).start()
        for fetch in fetches:
            fetch.start()
        normed[...] = jnp.zeros_like(normed)
        acc[...] = jnp.zeros_like(acc)
        weights.wait()
        w_t[...] = w_ref[:, channels:].T

    row_copy(step).wait()
    acc[...] += mm_nt(normed[:channels, :], normed[channels:, :])

    def project(block, _):
        return mm_nt(w_t[...], x_ref[step, block * KV_SUB : (block + 1) * KV_SUB, :])

    def normalize(block, both):
        shaped = both.reshape(2 * HEADS, HD, KV_SUB)
        center = shaped - jnp.sum(shaped, axis=1, keepdims=True) * (1.0 / HD)
        spread = jnp.sum(center * center, axis=1, keepdims=True) * (1.0 / HD) + EPSILON
        scaled = center * lax.rsqrt(spread)
        normed[:, block * KV_SUB : (block + 1) * KV_SUB] = scaled.reshape(2 * channels, KV_SUB).astype(BF16)

    skewed([project, normalize], x_ref.shape[1] // KV_SUB)

    @pl.when(step == pl.num_programs(0) - 1)
    def _():
        total = acc[...] + mm_nt(normed[:channels, :], normed[channels:, :])
        left = lax.broadcasted_iota(jnp.int32, (HD, 2 * HD), 1) < HD
        pairs = []
        for row in range(0, channels, 2 * HD):
            cols = slice(row, row + 2 * HD)
            pairs.append(jnp.where(left, total[row : row + HD, cols], total[row + HD : row + 2 * HD, cols]))
        odd = me_ref[0] == 1
        keep_ref[...] = jnp.where(odd, pairs[1], pairs[0])
        send_ref[...] = jnp.where(odd, pairs[0], pairs[1])
        for fetch in fetches:
            fetch.wait()


def query_kernel(x_ref, w_ref, out_ref):
    step = pl.program_id(0)
    out_ref[step] = mm(x_ref[step], w_ref[:, : x_ref.shape[2]]).astype(BF16)


def field_kernel(cells, me_ref, x_ref, kva_ref, kvb_ref, ask_ref, wa_ref, wi_ref, wo_ref, tab_ref, ang_ref, far_ref,
                 second_ref, keep_ref, send_ref, near_ref, scaled, spectra, terms, arrived):
    step = pl.program_id(0)
    rows = x_ref.shape[0]
    fetch = pltpu.make_async_copy(far_ref, near_ref, arrived)

    @pl.when(step == 0)
    def _():
        fetch.start()
        odd = me_ref[0] == 1
        mine, theirs = kva_ref[...] / cells, kvb_ref[...] / cells
        packed = (jnp.where(odd, theirs, mine), jnp.where(odd, mine, theirs))
        left = lax.broadcasted_iota(jnp.int32, (HD, 2 * HD), 1) < HD
        blank = jnp.zeros((HD, 2 * HD), F32)
        blocks = []
        for pair in range(HEADS // 2):
            part = packed[pair]
            for mine in (jnp.where(left, part, 0.0), jnp.where(left, 0.0, part)):
                line = [blank] * (HEADS // 2)
                line[pair] = mine
                blocks.append(jnp.concatenate(line, axis=1))
        scaled[...] = jnp.concatenate(blocks, axis=0).astype(BF16)

    columns = x_ref.shape[1]
    per_row = columns // SUB

    def place(block):
        return step * ROWS + block // per_row, slice(block % per_row * SUB, (block % per_row + 1) * SUB)

    def attend(block, _):
        row, here = place(block)
        return mm(ask_ref[row, here, :], scaled[...]).astype(BF16)

    def add(block, attended):
        row, here = place(block)
        return (x_ref[row, here, :].astype(F32) + mm(attended, wa_ref[...])).astype(BF16)

    def widen(block, first):
        return first, gelu(mm(first, wi_ref[...])).astype(BF16)

    def narrow(block, pair):
        row, here = place(block)
        first, hidden = pair
        second_ref[row, here, :] = (first.astype(F32) + mm(hidden, wo_ref[...])).astype(BF16)
        if block % per_row == per_row - 1:
            transform(row)

    def transform(row):
        at = pl.ds(pl.multiple_of(row * 2 * MW, 2 * MW), 2 * MW)
        split(spectra, at, mm(tab_ref[...], second_ref[row]))

    skewed([attend, add, widen, narrow], ROWS * per_row)

    @pl.when(step == pl.num_programs(0) - 1)
    def _():
        per_owner = keep_ref.shape[1]
        for kw in range(MW):
            spectrum = join(spectra, pl.ds(kw, 2 * rows, stride=MW), range(spectra.shape[0]))
            high = spectrum.astype(BF16)
            low = (spectrum - high.astype(F32)).astype(BF16)
            found = mm(ang_ref[me_ref[1]], jnp.concatenate([high, low, high], axis=0))
            at = rows_of(kw, per_owner, me_ref[0])
            split(terms, at, jnp.concatenate([found[:MH], found[MH:]], axis=1))
        fetch.wait()
        middle = MH * MW // 2
        for block in range(terms.shape[0]):
            here = slice(block * 128, (block + 1) * 128)
            keep_ref[:, :, here] = terms[block, :middle].reshape(keep_ref.shape[:2] + (128,))
            send_ref[:, :, here] = terms[block, middle:].astype(BF16).reshape(keep_ref.shape[:2] + (128,))


def mode_kernel(terms_ref, w_ref, out_ref):
    step = pl.program_id(0)
    group = 8
    channels = HEADS * HD
    rows = pl.ds(pl.multiple_of(step * group, group), group)
    coeff = jnp.sum(terms_ref[:, rows, :].astype(F32), axis=0).astype(BF16).astype(F32)
    re, im = coeff[:, :channels], coeff[:, channels:]
    lhs = jnp.concatenate(
        [jnp.concatenate([re, -im], axis=1), jnp.concatenate([im, re], axis=1)], axis=0
    ).astype(BF16)
    index = lax.broadcasted_iota(jnp.int32, (2 * group, channels), 0) % group
    mixed = jnp.zeros((2 * group, channels), F32)
    for m in range(group):
        mixed = jnp.where(index == m, mm(lhs, w_ref[step * group + m]), mixed)
    for copy in range(out_ref.shape[0]):
        out_ref[copy, rows, :channels] = mixed[:group].astype(BF16)
        out_ref[copy, rows, channels:] = mixed[group:].astype(BF16)


def last_kernel(cells, me_ref, second_ref, lo_ref, hi_ref, ws_ref, tab_ref, ang_ref, out_ref, mixed, back, held, sent):
    step = pl.program_id(0)
    channels = HEADS * HD
    rows = second_ref.shape[0]

    @pl.when(step == 0)
    def _():
        per_owner = lo_ref.shape[1]
        middle = MH * MW // 2
        split(mixed, slice(0, middle), lo_ref[...].astype(F32).reshape(middle, 2 * channels))
        split(mixed, slice(middle, None), hi_ref[...].astype(F32).reshape(middle, 2 * channels))
        for kw in range(MW):
            at = rows_of(kw, per_owner, me_ref[0])
            blocks = range(mixed.shape[0])
            re, im = join(mixed, at, blocks[: len(blocks) // 2]), join(mixed, at, blocks[len(blocks) // 2 :])
            both = jnp.concatenate([re, im], axis=0).astype(BF16)
            found = mm(ang_ref[me_ref[1]], jnp.concatenate([both, both], axis=0))
            split(back, pl.ds(kw, 2 * rows, stride=MW), found * ((2.0 if kw else 1.0) / cells))

    there = pl.ds(pl.multiple_of(step * 2 * MW, 2 * MW), 2 * MW)
    rhs = jnp.concatenate([ws_ref[...], join(back, there, range(back.shape[0])).astype(BF16)], axis=0)

    def both(block, _):
        here = slice(block * LAST_SUB, (block + 1) * LAST_SUB)
        return mm(jnp.concatenate([second_ref[step, here, :], tab_ref[here, :]], axis=1), rhs)

    blocks = second_ref.shape[1] // LAST_SUB

    def send(row, block):
        here = pl.ds(block * LAST_SUB, LAST_SUB)
        return pltpu.make_async_copy(held.at[row, here], out_ref.at[row, here], sent.at[row, block])

    def finish(block, value):
        held[step, block * LAST_SUB : (block + 1) * LAST_SUB, :] = gelu(value).astype(BF16)
        send(step, block).start()

    skewed([both, finish], blocks)

    @pl.when(step == pl.num_programs(0) - 1)
    def _():
        for row in range(rows):
            for block in range(blocks):
                send(row, block).wait()


def near(value):
    return pltpu.with_memory_space_constraint(value, pltpu.VMEM)


def away(value):
    return pltpu.with_memory_space_constraint(value, pltpu.HBM)


HERE = pl.BlockSpec(memory_space=pltpu.VMEM)


def local(field, w_qkv, w_attn, w_inner, w_outer, w_skip, w_modes):
    strip_rows, columns, channels = field.shape
    size = lax.axis_size("row")
    bits = size.bit_length() - 1
    assert size == 1 << bits and size > 1
    me = lax.axis_index("row")
    height = strip_rows * size
    cells = float(height * columns)
    per_owner = w_modes.shape[0]
    ids = jnp.stack([me & 1, me]).astype(jnp.int32)
    chips = [list(range(core, size, 2)) for core in (0, 1)]

    def swap(value, distance):
        return lax.ppermute(value, "row", [(i, i ^ distance) for i in range(size)])

    table = column_table(columns)
    wide = jnp.asarray(table.T, BF16)
    tall = jnp.asarray(table, BF16)
    ahead, behind = (jnp.asarray(t) for t in row_tables(size, strip_rows, per_owner))

    kv_shape = (HD, 2 * HD)
    hbm = pl.BlockSpec(memory_space=pltpu.HBM)
    keep, send, x_near, wq_near, wa_near, wi_near, wo_near = pl.pallas_call(
        kv_kernel,
        out_shape=[pltpu.VMEM(kv_shape, F32)] * 2 + [pltpu.VMEM(w.shape, BF16) for w in (field, w_qkv, w_attn, w_inner, w_outer)],
        grid_spec=pltpu.PrefetchScalarGridSpec(
            num_scalar_prefetch=1,
            grid=(strip_rows,),
            in_specs=[hbm] * 5,
            out_specs=[HERE] * 7,
            scratch_shapes=[
                pltpu.VMEM((2 * channels, channels), BF16),
                pltpu.VMEM((2 * channels, columns), BF16),
                pltpu.VMEM((channels, channels), F32),
                pltpu.SemaphoreType.DMA((4,)),
                pltpu.SemaphoreType.DMA((strip_rows,)),
            ],
        ),
        compiler_params=pltpu.CompilerParams(vmem_limit_bytes=12 << 20),
        name="kv",
    )(ids, away(field), away(w_qkv), away(w_attn), away(w_inner), away(w_outer))
    queries = pl.pallas_call(
        query_kernel,
        out_shape=pltpu.VMEM(field.shape, BF16),
        grid=(strip_rows,),
        in_specs=[HERE, HERE],
        out_specs=HERE,
        compiler_params=pltpu.CompilerParams(vmem_limit_bytes=4 << 20),
        cost_estimate=pl.CostEstimate(
            flops=2 * field.size * channels, bytes_accessed=4 * field.size, transcendentals=0
        ),
        name="qproj",
    )(near(x_near), near(wq_near))
    kv = keep + swap(send, 1)
    for b in range(1, bits, 2):
        steps = [1 << b] if b + 1 == bits else [1 << b, 2 << b, 3 << b]
        others = []
        for d in steps:
            others.append(swap(kv, d))
        kv = sum(others, kv)
    other = swap(kv, 1)

    half = (size // 2, per_owner, 2 * channels)
    mode_shape = (per_owner, 2 * channels, channels)
    second, keep, send, w_near = pl.pallas_call(
        functools.partial(field_kernel, cells),
        out_shape=[
            pltpu.VMEM(field.shape, BF16),
            pltpu.VMEM(half, F32),
            pltpu.VMEM(half, BF16),
            pltpu.VMEM(mode_shape, BF16),
        ],
        grid_spec=pltpu.PrefetchScalarGridSpec(
            num_scalar_prefetch=1,
            grid=(strip_rows // ROWS,),
            in_specs=[HERE] * 9 + [hbm],
            out_specs=[HERE, HERE, HERE, HERE],
            scratch_shapes=[
                pltpu.VMEM((channels, channels), BF16),
                pltpu.VMEM((channels // 128, strip_rows * 2 * MW, 128), F32),
                pltpu.VMEM((channels // 64, MH * MW, 128), F32),
                pltpu.SemaphoreType.DMA(()),
            ],
        ),
        compiler_params=pltpu.CompilerParams(vmem_limit_bytes=14 << 20),
        name="field",
    )(ids, *map(near, (x_near, kv, other, queries, wa_near, wi_near, wo_near, wide, ahead)), away(w_modes.reshape(mode_shape)))

    both = (keep + swap(send, 1).astype(F32)).astype(BF16)
    terms = lax.all_to_all(both, "row", 0, 0, axis_index_groups=chips, tiled=True)

    group = 8
    copies = pl.pallas_call(
        mode_kernel,
        out_shape=pltpu.VMEM(half, BF16),
        grid=(per_owner // group,),
        in_specs=[HERE, HERE],
        out_specs=HERE,
        compiler_params=pltpu.CompilerParams(vmem_limit_bytes=4 << 20),
        name="modes",
    )(near(terms), near(w_near))

    held = lax.all_to_all(copies, "row", 0, 0, axis_index_groups=chips, tiled=True)
    far = swap(held, 1)

    return pl.pallas_call(
        functools.partial(last_kernel, cells),
        out_shape=jax.ShapeDtypeStruct(field.shape, BF16),
        grid_spec=pltpu.PrefetchScalarGridSpec(
            num_scalar_prefetch=1,
            grid=(strip_rows,),
            in_specs=[HERE] * 6,
            out_specs=hbm,
            scratch_shapes=[
                pltpu.VMEM((channels // 64, MH * MW, 128), F32),
                pltpu.VMEM((channels // 128, strip_rows * 2 * MW, 128), F32),
                pltpu.VMEM(field.shape, BF16),
                pltpu.SemaphoreType.DMA((strip_rows, columns // LAST_SUB)),
            ],
        ),
        compiler_params=pltpu.CompilerParams(vmem_limit_bytes=12 << 20),
        name="last",
    )(ids, *map(near, (second, held, far, w_skip, tall, behind)))


def solution(mesh):
    placed = (P(("grp", "row"), None, None), P(), P(), P(), P(), P(), P("row", None, None, None))
    return jax.shard_map(local, mesh=mesh, in_specs=placed, out_specs=P(("grp", "row"), None, None), check_vma=False)
```

```python
import functools

import jax
import jax.numpy as jnp
import numpy as np
from jax import lax
from jax.experimental import pallas as pl
from jax.experimental.pallas import tpu as pltpu
from jax.sharding import PartitionSpec as P

HEADS = 4
HD = 64
MH = 32
MW = 16
EPSILON = 1e-05
SUB = 512
KV_SUB = 256
LAST_SUB = 1024
LAST_ROWS = 4
ROWS = 2
F32 = jnp.float32
BF16 = jnp.bfloat16


def mm(a, b):
    return jnp.dot(a, b, preferred_element_type=F32)


def mm_nt(a, b):
    return lax.dot_general(a, b, (((1,), (1,)), ((), ())), preferred_element_type=F32)


def gelu(x):
    half = 0.5 * x
    return half + half * lax.erf(x * 0.7071067811865476)


def skewed(stages, count):
    held = [None] * count
    for at in range(count + len(stages) - 1):
        for k in reversed(range(len(stages))):
            if 0 <= at - k < count:
                held[at - k] = stages[k](at - k, held[at - k])


def column_table(columns):
    turns = np.arange(columns)[:, None] * np.arange(MW)[None, :] % columns
    angle = turns * (2 * np.pi / columns)
    return np.concatenate([np.cos(angle), -np.sin(angle)], axis=1)


def split(ref, at, value):
    for block in range(value.shape[1] // 128):
        ref[block, at, :] = value[:, block * 128 : (block + 1) * 128]


def join(ref, at, blocks):
    return jnp.concatenate([ref[block, at, :] for block in blocks], axis=1)


def halves(value):
    high = value.astype(BF16)
    return high, (value - np.asarray(high, np.float64)).astype(BF16)


def placing(size, per_owner, odd):
    if per_owner < MW:
        return list(range(MH))
    group = per_owner // MW
    owners = [*range(odd, size, 2), *range(1 - odd, size, 2)]
    return [owner * group + k for owner in owners for k in range(group)]


def rows_of(kw, per_owner, odd):
    if per_owner >= MW:
        return pl.ds(kw, MH, stride=MW)
    part = kw // per_owner
    first = ((part & 1) ^ odd) * (MH * MW // 2) + part // 2 * per_owner + kw % per_owner
    return pl.ds(first, MH, stride=MW // 2)


def row_tables(size, strip_rows, per_owner):
    height = size * strip_rows
    ahead, back = [], []
    for me in range(size):
        order = np.array(placing(size, per_owner, me & 1))
        freqs = np.where(order < MH // 2, order, order - MH + height)
        angle = freqs[:, None] * (me * strip_rows + np.arange(strip_rows))[None, :] % height * (2 * np.pi / height)
        cos, sin = np.cos(angle), np.sin(angle)
        real = np.stack([cos, sin], axis=2).reshape(MH, -1)
        imag = np.stack([-sin, cos], axis=2).reshape(MH, -1)
        high, low = halves(np.concatenate([real, imag]))
        ahead.append(np.concatenate([high, high, low], axis=1))
        real = np.concatenate([cos, -sin]).T
        imag = np.concatenate([sin, cos]).T
        back.append(np.concatenate(halves(np.stack([real, imag], axis=1).reshape(2 * strip_rows, -1)), axis=1))
    return np.stack(ahead), np.stack(back)


def kv_kernel(me_ref, far_ref, w_far, wa_ref, wi_ref, wo_ref, keep_ref, send_ref, x_ref, w_ref, wa_near, wi_near, wo_near,
              w_t, raw, normed, acc, arrived, landed):
    step = pl.program_id(0)
    channels = HEADS * HD
    fetches = [
        pltpu.make_async_copy(far, to, arrived.at[i])
        for i, (far, to) in enumerate(((wa_ref, wa_near), (wi_ref, wi_near), (wo_ref, wo_near)))
    ]

    def row_copy(row):
        return pltpu.make_async_copy(far_ref.at[row], x_ref.at[row], landed.at[row])

    @pl.when(step == 0)
    def _():
        weights = pltpu.make_async_copy(w_far, w_ref, arrived.at[3])
        weights.start()
        for row in range(x_ref.shape[0]):
            row_copy(row).start()
        for fetch in fetches:
            fetch.start()
        raw[...] = jnp.zeros_like(raw)
        normed[...] = jnp.zeros_like(normed)
        acc[...] = jnp.zeros_like(acc)
        weights.wait()
        w_t[...] = w_ref[:, channels:].T

    blocks = x_ref.shape[1] // KV_SUB

    def project(block):
        return mm_nt(w_t[...], x_ref[step, block * KV_SUB : (block + 1) * KV_SUB, :])

    def normalize(block, both):
        shaped = both.reshape(2 * HEADS, HD, KV_SUB)
        center = shaped - jnp.sum(shaped, axis=1, keepdims=True) * (1.0 / HD)
        spread = jnp.sum(center * center, axis=1, keepdims=True) * (1.0 / HD) + EPSILON
        scaled = center * lax.rsqrt(spread)
        normed[:, block * KV_SUB : (block + 1) * KV_SUB] = scaled.reshape(2 * channels, KV_SUB).astype(BF16)

    row_copy(step).wait()
    here = project(0)
    normalize(blocks - 1, raw[...])
    acc[...] += mm_nt(normed[:channels, :], normed[channels:, :])
    ahead = project(1)
    for block in range(blocks - 1):
        normalize(block, here)
        here = ahead
        if block + 2 < blocks:
            ahead = project(block + 2)
    raw[...] = here

    @pl.when(step == pl.num_programs(0) - 1)
    def _():
        normalize(blocks - 1, raw[...])
        total = acc[...] + mm_nt(normed[:channels, :], normed[channels:, :])
        left = lax.broadcasted_iota(jnp.int32, (HD, 2 * HD), 1) < HD
        pairs = []
        for row in range(0, channels, 2 * HD):
            cols = slice(row, row + 2 * HD)
            pairs.append(jnp.where(left, total[row : row + HD, cols], total[row + HD : row + 2 * HD, cols]))
        odd = me_ref[0] == 1
        keep_ref[...] = jnp.where(odd, pairs[1], pairs[0])
        send_ref[...] = jnp.where(odd, pairs[0], pairs[1])
        for fetch in fetches:
            fetch.wait()


def query_kernel(x_ref, w_ref, out_ref):
    step = pl.program_id(0)
    out_ref[step] = mm(x_ref[step], w_ref[:, : x_ref.shape[2]]).astype(BF16)


def field_kernel(cells, me_ref, x_ref, kva_ref, kvb_ref, ask_ref, wa_ref, wi_ref, wo_ref, tab_ref, ang_ref, far_ref,
                 second_ref, keep_ref, send_ref, near_ref, scaled, spectra, terms, arrived):
    step = pl.program_id(0)
    rows = x_ref.shape[0]
    fetch = pltpu.make_async_copy(far_ref, near_ref, arrived)

    @pl.when(step == 0)
    def _():
        fetch.start()
        odd = me_ref[0] == 1
        mine, theirs = kva_ref[...] / cells, kvb_ref[...] / cells
        packed = (jnp.where(odd, theirs, mine), jnp.where(odd, mine, theirs))
        left = lax.broadcasted_iota(jnp.int32, (HD, 2 * HD), 1) < HD
        blank = jnp.zeros((HD, 2 * HD), F32)
        blocks = []
        for pair in range(HEADS // 2):
            part = packed[pair]
            for mine in (jnp.where(left, part, 0.0), jnp.where(left, 0.0, part)):
                line = [blank] * (HEADS // 2)
                line[pair] = mine
                blocks.append(jnp.concatenate(line, axis=1))
        scaled[...] = jnp.concatenate(blocks, axis=0).astype(BF16)

    columns = x_ref.shape[1]
    per_row = columns // SUB

    def place(block):
        return step * ROWS + block // per_row, slice(block % per_row * SUB, (block % per_row + 1) * SUB)

    def attend(block, _):
        row, here = place(block)
        return mm(ask_ref[row, here, :], scaled[...]).astype(BF16)

    def add(block, attended):
        row, here = place(block)
        return (x_ref[row, here, :].astype(F32) + mm(attended, wa_ref[...])).astype(BF16)

    def widen(block, first):
        return first, gelu(mm(first, wi_ref[...])).astype(BF16)

    def narrow(block, pair):
        row, here = place(block)
        first, hidden = pair
        second_ref[row, here, :] = (first.astype(F32) + mm(hidden, wo_ref[...])).astype(BF16)
        if block % per_row == per_row - 1:
            transform(row)

    def transform(row):
        at = pl.ds(pl.multiple_of(row * 2 * MW, 2 * MW), 2 * MW)
        split(spectra, at, mm(tab_ref[...], second_ref[row]))

    skewed([attend, add, widen, narrow], ROWS * per_row)

    @pl.when(step == pl.num_programs(0) - 1)
    def _():
        per_owner = keep_ref.shape[1]
        for kw in range(MW):
            spectrum = join(spectra, pl.ds(kw, 2 * rows, stride=MW), range(spectra.shape[0]))
            high = spectrum.astype(BF16)
            low = (spectrum - high.astype(F32)).astype(BF16)
            found = mm(ang_ref[me_ref[1]], jnp.concatenate([high, low, high], axis=0))
            at = rows_of(kw, per_owner, me_ref[0])
            split(terms, at, jnp.concatenate([found[:MH], found[MH:]], axis=1))
        fetch.wait()
        middle = MH * MW // 2
        for block in range(terms.shape[0]):
            here = slice(block * 128, (block + 1) * 128)
            keep_ref[:, :, here] = terms[block, :middle].reshape(keep_ref.shape[:2] + (128,))
            send_ref[:, :, here] = terms[block, middle:].astype(BF16).reshape(keep_ref.shape[:2] + (128,))


def mode_kernel(terms_ref, w_ref, out_ref):
    step = pl.program_id(0)
    group = 8
    channels = HEADS * HD
    rows = pl.ds(pl.multiple_of(step * group, group), group)
    coeff = jnp.sum(terms_ref[:, rows, :].astype(F32), axis=0).astype(BF16).astype(F32)
    re, im = coeff[:, :channels], coeff[:, channels:]
    lhs = jnp.concatenate(
        [jnp.concatenate([re, -im], axis=1), jnp.concatenate([im, re], axis=1)], axis=0
    ).astype(BF16)
    index = lax.broadcasted_iota(jnp.int32, (2 * group, channels), 0) % group
    mixed = jnp.zeros((2 * group, channels), F32)
    for m in range(group):
        mixed = jnp.where(index == m, mm(lhs, w_ref[step * group + m]), mixed)
    for copy in range(out_ref.shape[0]):
        out_ref[copy, rows, :channels] = mixed[:group].astype(BF16)
        out_ref[copy, rows, channels:] = mixed[group:].astype(BF16)


def last_kernel(cells, me_ref, second_ref, lo_ref, hi_ref, ws_ref, tab_ref, ang_ref, out_ref, mixed, back, held, sent):
    step = pl.program_id(0)
    channels = HEADS * HD
    rows = second_ref.shape[0]

    @pl.when(step == 0)
    def _():
        per_owner = lo_ref.shape[1]
        middle = MH * MW // 2
        split(mixed, slice(0, middle), lo_ref[...].astype(F32).reshape(middle, 2 * channels))
        split(mixed, slice(middle, None), hi_ref[...].astype(F32).reshape(middle, 2 * channels))
        for kw in range(MW):
            at = rows_of(kw, per_owner, me_ref[0])
            blocks = range(mixed.shape[0])
            re, im = join(mixed, at, blocks[: len(blocks) // 2]), join(mixed, at, blocks[len(blocks) // 2 :])
            both = jnp.concatenate([re, im], axis=0).astype(BF16)
            found = mm(ang_ref[me_ref[1]], jnp.concatenate([both, both], axis=0))
            split(back, pl.ds(kw, 2 * rows, stride=MW), found * ((2.0 if kw else 1.0) / cells))

    parts = second_ref.shape[1] // LAST_SUB

    def send(row, part):
        here = pl.ds(part * LAST_SUB, LAST_SUB)
        return pltpu.make_async_copy(held.at[row, here], out_ref.at[row, here], sent.at[row, part])

    def place(block):
        return step * LAST_ROWS + block // parts, block % parts

    def both(block, _):
        row, part = place(block)
        here = slice(part * LAST_SUB, (part + 1) * LAST_SUB)
        there = pl.ds(pl.multiple_of(row * 2 * MW, 2 * MW), 2 * MW)
        rhs = jnp.concatenate([ws_ref[...], join(back, there, range(back.shape[0])).astype(BF16)], axis=0)
        return mm(jnp.concatenate([second_ref[row, here, :], tab_ref[here, :]], axis=1), rhs)

    def finish(block, value):
        row, part = place(block)
        held[row, part * LAST_SUB : (part + 1) * LAST_SUB, :] = gelu(value).astype(BF16)
        send(row, part).start()

    skewed([both, finish], LAST_ROWS * parts)

    @pl.when(step == pl.num_programs(0) - 1)
    def _():
        for row in range(rows):
            for part in range(parts):
                send(row, part).wait()


def near(value):
    return pltpu.with_memory_space_constraint(value, pltpu.VMEM)


def away(value):
    return pltpu.with_memory_space_constraint(value, pltpu.HBM)


HERE = pl.BlockSpec(memory_space=pltpu.VMEM)


def local(field, w_qkv, w_attn, w_inner, w_outer, w_skip, w_modes):
    strip_rows, columns, channels = field.shape
    size = lax.axis_size("row")
    bits = size.bit_length() - 1
    assert size == 1 << bits and size > 1
    me = lax.axis_index("row")
    height = strip_rows * size
    cells = float(height * columns)
    per_owner = w_modes.shape[0]
    ids = jnp.stack([me & 1, me]).astype(jnp.int32)
    chips = [list(range(core, size, 2)) for core in (0, 1)]

    def swap(value, distance):
        return lax.ppermute(value, "row", [(i, i ^ distance) for i in range(size)])

    table = column_table(columns)
    wide = jnp.asarray(table.T, BF16)
    tall = jnp.asarray(table, BF16)
    ahead, behind = (jnp.asarray(t) for t in row_tables(size, strip_rows, per_owner))

    kv_shape = (HD, 2 * HD)
    hbm = pl.BlockSpec(memory_space=pltpu.HBM)
    keep, send, x_near, wq_near, wa_near, wi_near, wo_near = pl.pallas_call(
        kv_kernel,
        out_shape=[pltpu.VMEM(kv_shape, F32)] * 2 + [pltpu.VMEM(w.shape, BF16) for w in (field, w_qkv, w_attn, w_inner, w_outer)],
        grid_spec=pltpu.PrefetchScalarGridSpec(
            num_scalar_prefetch=1,
            grid=(strip_rows,),
            in_specs=[hbm] * 5,
            out_specs=[HERE] * 7,
            scratch_shapes=[
                pltpu.VMEM((2 * channels, channels), BF16),
                pltpu.VMEM((2 * channels, KV_SUB), F32),
                pltpu.VMEM((2 * channels, columns), BF16),
                pltpu.VMEM((channels, channels), F32),
                pltpu.SemaphoreType.DMA((4,)),
                pltpu.SemaphoreType.DMA((strip_rows,)),
            ],
        ),
        compiler_params=pltpu.CompilerParams(vmem_limit_bytes=12 << 20),
        name="kv",
    )(ids, away(field), away(w_qkv), away(w_attn), away(w_inner), away(w_outer))
    queries = pl.pallas_call(
        query_kernel,
        out_shape=pltpu.VMEM(field.shape, BF16),
        grid=(strip_rows,),
        in_specs=[HERE, HERE],
        out_specs=HERE,
        compiler_params=pltpu.CompilerParams(vmem_limit_bytes=4 << 20),
        cost_estimate=pl.CostEstimate(
            flops=2 * field.size * channels, bytes_accessed=4 * field.size, transcendentals=0
        ),
        name="qproj",
    )(near(x_near), near(wq_near))
    kv = keep + swap(send, 1)
    for b in range(1, bits, 2):
        steps = [1 << b] if b + 1 == bits else [1 << b, 2 << b, 3 << b]
        others = []
        for d in steps:
            others.append(swap(kv, d))
        kv = sum(others, kv)
    other = swap(kv, 1)

    half = (size // 2, per_owner, 2 * channels)
    mode_shape = (per_owner, 2 * channels, channels)
    second, keep, send, w_near = pl.pallas_call(
        functools.partial(field_kernel, cells),
        out_shape=[
            pltpu.VMEM(field.shape, BF16),
            pltpu.VMEM(half, F32),
            pltpu.VMEM(half, BF16),
            pltpu.VMEM(mode_shape, BF16),
        ],
        grid_spec=pltpu.PrefetchScalarGridSpec(
            num_scalar_prefetch=1,
            grid=(strip_rows // ROWS,),
            in_specs=[HERE] * 9 + [hbm],
            out_specs=[HERE, HERE, HERE, HERE],
            scratch_shapes=[
                pltpu.VMEM((channels, channels), BF16),
                pltpu.VMEM((channels // 128, strip_rows * 2 * MW, 128), F32),
                pltpu.VMEM((channels // 64, MH * MW, 128), F32),
                pltpu.SemaphoreType.DMA(()),
            ],
        ),
        compiler_params=pltpu.CompilerParams(vmem_limit_bytes=14 << 20),
        name="field",
    )(ids, *map(near, (x_near, kv, other, queries, wa_near, wi_near, wo_near, wide, ahead)), away(w_modes.reshape(mode_shape)))

    both = (keep + swap(send, 1).astype(F32)).astype(BF16)
    terms = lax.all_to_all(both, "row", 0, 0, axis_index_groups=chips, tiled=True)

    group = 8
    copies = pl.pallas_call(
        mode_kernel,
        out_shape=pltpu.VMEM(half, BF16),
        grid=(per_owner // group,),
        in_specs=[HERE, HERE],
        out_specs=HERE,
        compiler_params=pltpu.CompilerParams(vmem_limit_bytes=4 << 20),
        name="modes",
    )(near(terms), near(w_near))

    held = lax.all_to_all(copies, "row", 0, 0, axis_index_groups=chips, tiled=True)
    far = swap(held, 1)

    return pl.pallas_call(
        functools.partial(last_kernel, cells),
        out_shape=jax.ShapeDtypeStruct(field.shape, BF16),
        grid_spec=pltpu.PrefetchScalarGridSpec(
            num_scalar_prefetch=1,
            grid=(strip_rows // LAST_ROWS,),
            in_specs=[HERE] * 6,
            out_specs=hbm,
            scratch_shapes=[
                pltpu.VMEM((channels // 64, MH * MW, 128), F32),
                pltpu.VMEM((channels // 128, strip_rows * 2 * MW, 128), F32),
                pltpu.VMEM(field.shape, BF16),
                pltpu.SemaphoreType.DMA((strip_rows, columns // LAST_SUB)),
            ],
        ),
        compiler_params=pltpu.CompilerParams(vmem_limit_bytes=12 << 20),
        name="last",
    )(ids, *map(near, (second, held, far, w_skip, tall, behind)))


def solution(mesh):
    placed = (P(("grp", "row"), None, None), P(), P(), P(), P(), P(), P("row", None, None, None))
    return jax.shard_map(local, mesh=mesh, in_specs=placed, out_specs=P(("grp", "row"), None, None), check_vma=False)
```

```python
import functools

import jax
import jax.numpy as jnp
import numpy as np
from jax import lax
from jax.experimental import pallas as pl
from jax.experimental.pallas import tpu as pltpu
from jax.sharding import PartitionSpec as P

HEADS = 4
HD = 64
MH = 32
MW = 16
EPSILON = 1e-05
SUB = 512
KV_SUB = 256
LAST_SUB = 512
LAST_ROWS = 8
ROWS = 4
F32 = jnp.float32
BF16 = jnp.bfloat16


def mm(a, b):
    return jnp.dot(a, b, preferred_element_type=F32)


def mm_nt(a, b):
    return lax.dot_general(a, b, (((1,), (1,)), ((), ())), preferred_element_type=F32)


def gelu(x):
    half = 0.5 * x
    return half + half * lax.erf(x * 0.7071067811865476)


def skewed(stages, count):
    held = [None] * count
    for at in range(count + len(stages) - 1):
        for k in reversed(range(len(stages))):
            if 0 <= at - k < count:
                held[at - k] = stages[k](at - k, held[at - k])


def column_table(columns):
    turns = np.arange(columns)[:, None] * np.arange(MW)[None, :] % columns
    angle = turns * (2 * np.pi / columns)
    return np.concatenate([np.cos(angle), -np.sin(angle)], axis=1)


def split(ref, at, value):
    for block in range(value.shape[1] // 128):
        ref[block, at, :] = value[:, block * 128 : (block + 1) * 128]


def join(ref, at, blocks):
    return jnp.concatenate([ref[block, at, :] for block in blocks], axis=1)


def halves(value):
    high = value.astype(BF16)
    return high, (value - np.asarray(high, np.float64)).astype(BF16)


def placing(size, per_owner, odd):
    if per_owner < MW:
        return list(range(MH))
    group = per_owner // MW
    owners = [*range(odd, size, 2), *range(1 - odd, size, 2)]
    return [owner * group + k for owner in owners for k in range(group)]


def rows_of(kw, per_owner, odd):
    if per_owner >= MW:
        return pl.ds(kw, MH, stride=MW)
    part = kw // per_owner
    first = ((part & 1) ^ odd) * (MH * MW // 2) + part // 2 * per_owner + kw % per_owner
    return pl.ds(first, MH, stride=MW // 2)


def row_tables(size, strip_rows, per_owner):
    height = size * strip_rows
    ahead, back = [], []
    for me in range(size):
        order = np.array(placing(size, per_owner, me & 1))
        freqs = np.where(order < MH // 2, order, order - MH + height)
        angle = freqs[:, None] * (me * strip_rows + np.arange(strip_rows))[None, :] % height * (2 * np.pi / height)
        cos, sin = np.cos(angle), np.sin(angle)
        real = np.stack([cos, sin], axis=2).reshape(MH, -1)
        imag = np.stack([-sin, cos], axis=2).reshape(MH, -1)
        high, low = halves(np.concatenate([real, imag]))
        ahead.append(np.concatenate([high, high, low], axis=1))
        real = np.concatenate([cos, -sin]).T
        imag = np.concatenate([sin, cos]).T
        back.append(np.concatenate(halves(np.stack([real, imag], axis=1).reshape(2 * strip_rows, -1)), axis=1))
    return np.stack(ahead), np.stack(back)


def kv_kernel(me_ref, far_ref, w_far, wa_ref, wi_ref, wo_ref, keep_ref, send_ref, x_ref, w_ref, wa_near, wi_near, wo_near,
              w_t, raw, normed, acc, arrived, landed):
    step = pl.program_id(0)
    channels = HEADS * HD
    fetches = [
        pltpu.make_async_copy(far, to, arrived.at[i])
        for i, (far, to) in enumerate(((wa_ref, wa_near), (wi_ref, wi_near), (wo_ref, wo_near)))
    ]

    def row_copy(row):
        return pltpu.make_async_copy(far_ref.at[row], x_ref.at[row], landed.at[row])

    @pl.when(step == 0)
    def _():
        weights = pltpu.make_async_copy(w_far, w_ref, arrived.at[3])
        weights.start()
        for row in range(x_ref.shape[0]):
            row_copy(row).start()
        for fetch in fetches:
            fetch.start()
        raw[...] = jnp.zeros_like(raw)
        normed[...] = jnp.zeros_like(normed)
        acc[...] = jnp.zeros_like(acc)
        weights.wait()
        w_t[...] = w_ref[:, channels:].T

    blocks = x_ref.shape[1] // KV_SUB

    def project(block):
        return mm_nt(w_t[...], x_ref[step, block * KV_SUB : (block + 1) * KV_SUB, :])

    def normalize(block, both):
        shaped = both.reshape(2 * HEADS, HD, KV_SUB)
        center = shaped - jnp.sum(shaped, axis=1, keepdims=True) * (1.0 / HD)
        spread = jnp.sum(center * center, axis=1, keepdims=True) * (1.0 / HD) + EPSILON
        scaled = center * lax.rsqrt(spread)
        normed[:, block * KV_SUB : (block + 1) * KV_SUB] = scaled.reshape(2 * channels, KV_SUB).astype(BF16)

    row_copy(step).wait()
    here = project(0)
    normalize(blocks - 1, raw[...])
    acc[...] += mm_nt(normed[:channels, :], normed[channels:, :])
    ahead = project(1)
    for block in range(blocks - 1):
        normalize(block, here)
        here = ahead
        if block + 2 < blocks:
            ahead = project(block + 2)
    raw[...] = here

    @pl.when(step == pl.num_programs(0) - 1)
    def _():
        normalize(blocks - 1, raw[...])
        total = acc[...] + mm_nt(normed[:channels, :], normed[channels:, :])
        left = lax.broadcasted_iota(jnp.int32, (HD, 2 * HD), 1) < HD
        pairs = []
        for row in range(0, channels, 2 * HD):
            cols = slice(row, row + 2 * HD)
            pairs.append(jnp.where(left, total[row : row + HD, cols], total[row + HD : row + 2 * HD, cols]))
        odd = me_ref[0] == 1
        keep_ref[...] = jnp.where(odd, pairs[1], pairs[0])
        send_ref[...] = jnp.where(odd, pairs[0], pairs[1])
        for fetch in fetches:
            fetch.wait()


def query_kernel(x_ref, w_ref, out_ref):
    step = pl.program_id(0)
    out_ref[step] = mm(x_ref[step], w_ref[:, : x_ref.shape[2]]).astype(BF16)


def field_kernel(cells, me_ref, x_ref, kva_ref, kvb_ref, ask_ref, wa_ref, wi_ref, wo_ref, tab_ref, ang_ref, far_ref,
                 second_ref, keep_ref, send_ref, near_ref, scaled, spectra, terms, arrived):
    step = pl.program_id(0)
    rows = x_ref.shape[0]
    fetch = pltpu.make_async_copy(far_ref, near_ref, arrived)

    @pl.when(step == 0)
    def _():
        fetch.start()
        odd = me_ref[0] == 1
        mine, theirs = kva_ref[...] / cells, kvb_ref[...] / cells
        packed = (jnp.where(odd, theirs, mine), jnp.where(odd, mine, theirs))
        left = lax.broadcasted_iota(jnp.int32, (HD, 2 * HD), 1) < HD
        blank = jnp.zeros((HD, 2 * HD), F32)
        blocks = []
        for pair in range(HEADS // 2):
            part = packed[pair]
            for mine in (jnp.where(left, part, 0.0), jnp.where(left, 0.0, part)):
                line = [blank] * (HEADS // 2)
                line[pair] = mine
                blocks.append(jnp.concatenate(line, axis=1))
        scaled[...] = jnp.concatenate(blocks, axis=0).astype(BF16)

    columns = x_ref.shape[1]
    per_row = columns // SUB

    def place(block):
        return step * ROWS + block // per_row, slice(block % per_row * SUB, (block % per_row + 1) * SUB)

    def attend(block, _):
        row, here = place(block)
        return mm(ask_ref[row, here, :], scaled[...]).astype(BF16)

    def add(block, attended):
        row, here = place(block)
        return (x_ref[row, here, :].astype(F32) + mm(attended, wa_ref[...])).astype(BF16)

    def widen(block, first):
        return first, gelu(mm(first, wi_ref[...])).astype(BF16)

    def narrow(block, pair):
        row, here = place(block)
        first, hidden = pair
        second_ref[row, here, :] = (first.astype(F32) + mm(hidden, wo_ref[...])).astype(BF16)
        if block % per_row == per_row - 1:
            transform(row)

    def transform(row):
        at = pl.ds(pl.multiple_of(row * 2 * MW, 2 * MW), 2 * MW)
        split(spectra, at, mm(tab_ref[...], second_ref[row]))

    skewed([attend, add, widen, narrow], ROWS * per_row)

    @pl.when(step == pl.num_programs(0) - 1)
    def _():
        per_owner = keep_ref.shape[1]
        for kw in range(MW):
            spectrum = join(spectra, pl.ds(kw, 2 * rows, stride=MW), range(spectra.shape[0]))
            high = spectrum.astype(BF16)
            low = (spectrum - high.astype(F32)).astype(BF16)
            found = mm(ang_ref[me_ref[1]], jnp.concatenate([high, low, high], axis=0))
            at = rows_of(kw, per_owner, me_ref[0])
            split(terms, at, jnp.concatenate([found[:MH], found[MH:]], axis=1))
        fetch.wait()
        middle = MH * MW // 2
        for block in range(terms.shape[0]):
            here = slice(block * 128, (block + 1) * 128)
            keep_ref[:, :, here] = terms[block, :middle].reshape(keep_ref.shape[:2] + (128,))
            send_ref[:, :, here] = terms[block, middle:].astype(BF16).reshape(keep_ref.shape[:2] + (128,))


def mode_kernel(terms_ref, w_ref, out_ref):
    step = pl.program_id(0)
    group = 8
    channels = HEADS * HD
    rows = pl.ds(pl.multiple_of(step * group, group), group)
    coeff = jnp.sum(terms_ref[:, rows, :].astype(F32), axis=0).astype(BF16).astype(F32)
    re, im = coeff[:, :channels], coeff[:, channels:]
    lhs = jnp.concatenate(
        [jnp.concatenate([re, -im], axis=1), jnp.concatenate([im, re], axis=1)], axis=0
    ).astype(BF16)
    index = lax.broadcasted_iota(jnp.int32, (2 * group, channels), 0) % group
    mixed = jnp.zeros((2 * group, channels), F32)
    for m in range(group):
        mixed = jnp.where(index == m, mm(lhs, w_ref[step * group + m]), mixed)
    for copy in range(out_ref.shape[0]):
        out_ref[copy, rows, :channels] = mixed[:group].astype(BF16)
        out_ref[copy, rows, channels:] = mixed[group:].astype(BF16)


def last_kernel(cells, me_ref, second_ref, lo_ref, hi_ref, ws_ref, tab_ref, ang_ref, out_ref, mixed, back, held, sent):
    step = pl.program_id(0)
    channels = HEADS * HD
    rows = second_ref.shape[0]

    @pl.when(step == 0)
    def _():
        per_owner = lo_ref.shape[1]
        middle = MH * MW // 2
        split(mixed, slice(0, middle), lo_ref[...].astype(F32).reshape(middle, 2 * channels))
        split(mixed, slice(middle, None), hi_ref[...].astype(F32).reshape(middle, 2 * channels))
        for kw in range(MW):
            at = rows_of(kw, per_owner, me_ref[0])
            blocks = range(mixed.shape[0])
            re, im = join(mixed, at, blocks[: len(blocks) // 2]), join(mixed, at, blocks[len(blocks) // 2 :])
            both = jnp.concatenate([re, im], axis=0).astype(BF16)
            found = mm(ang_ref[me_ref[1]], jnp.concatenate([both, both], axis=0))
            split(back, pl.ds(kw, 2 * rows, stride=MW), found * ((2.0 if kw else 1.0) / cells))

    parts = second_ref.shape[1] // LAST_SUB

    def send(row, part):
        here = pl.ds(part * LAST_SUB, LAST_SUB)
        return pltpu.make_async_copy(held.at[row, here], out_ref.at[row, here], sent.at[row, part])

    def place(block):
        return step * LAST_ROWS + block // parts, block % parts

    def both(block, _):
        row, part = place(block)
        here = slice(part * LAST_SUB, (part + 1) * LAST_SUB)
        there = pl.ds(pl.multiple_of(row * 2 * MW, 2 * MW), 2 * MW)
        rhs = jnp.concatenate([ws_ref[...], join(back, there, range(back.shape[0])).astype(BF16)], axis=0)
        return mm(jnp.concatenate([second_ref[row, here, :], tab_ref[here, :]], axis=1), rhs)

    def finish(block, value):
        row, part = place(block)
        held[row, part * LAST_SUB : (part + 1) * LAST_SUB, :] = gelu(value).astype(BF16)
        send(row, part).start()

    skewed([both, finish], LAST_ROWS * parts)

    @pl.when(step == pl.num_programs(0) - 1)
    def _():
        for row in range(rows):
            for part in range(parts):
                send(row, part).wait()


def near(value):
    return pltpu.with_memory_space_constraint(value, pltpu.VMEM)


def away(value):
    return pltpu.with_memory_space_constraint(value, pltpu.HBM)


HERE = pl.BlockSpec(memory_space=pltpu.VMEM)


def local(field, w_qkv, w_attn, w_inner, w_outer, w_skip, w_modes):
    strip_rows, columns, channels = field.shape
    size = lax.axis_size("row")
    bits = size.bit_length() - 1
    assert size == 1 << bits and size > 1
    me = lax.axis_index("row")
    height = strip_rows * size
    cells = float(height * columns)
    per_owner = w_modes.shape[0]
    ids = jnp.stack([me & 1, me]).astype(jnp.int32)
    chips = [list(range(core, size, 2)) for core in (0, 1)]

    def swap(value, distance):
        return lax.ppermute(value, "row", [(i, i ^ distance) for i in range(size)])

    table = column_table(columns)
    wide = jnp.asarray(table.T, BF16)
    tall = jnp.asarray(table, BF16)
    ahead, behind = (jnp.asarray(t) for t in row_tables(size, strip_rows, per_owner))

    kv_shape = (HD, 2 * HD)
    hbm = pl.BlockSpec(memory_space=pltpu.HBM)
    keep, send, x_near, wq_near, wa_near, wi_near, wo_near = pl.pallas_call(
        kv_kernel,
        out_shape=[pltpu.VMEM(kv_shape, F32)] * 2 + [pltpu.VMEM(w.shape, BF16) for w in (field, w_qkv, w_attn, w_inner, w_outer)],
        grid_spec=pltpu.PrefetchScalarGridSpec(
            num_scalar_prefetch=1,
            grid=(strip_rows,),
            in_specs=[hbm] * 5,
            out_specs=[HERE] * 7,
            scratch_shapes=[
                pltpu.VMEM((2 * channels, channels), BF16),
                pltpu.VMEM((2 * channels, KV_SUB), F32),
                pltpu.VMEM((2 * channels, columns), BF16),
                pltpu.VMEM((channels, channels), F32),
                pltpu.SemaphoreType.DMA((4,)),
                pltpu.SemaphoreType.DMA((strip_rows,)),
            ],
        ),
        compiler_params=pltpu.CompilerParams(vmem_limit_bytes=12 << 20),
        name="kv",
    )(ids, away(field), away(w_qkv), away(w_attn), away(w_inner), away(w_outer))
    queries = pl.pallas_call(
        query_kernel,
        out_shape=pltpu.VMEM(field.shape, BF16),
        grid=(strip_rows,),
        in_specs=[HERE, HERE],
        out_specs=HERE,
        compiler_params=pltpu.CompilerParams(vmem_limit_bytes=4 << 20),
        cost_estimate=pl.CostEstimate(
            flops=2 * field.size * channels, bytes_accessed=4 * field.size, transcendentals=0
        ),
        name="qproj",
    )(near(x_near), near(wq_near))
    kv = keep + swap(send, 1)
    for b in range(1, bits, 2):
        steps = [1 << b] if b + 1 == bits else [1 << b, 2 << b, 3 << b]
        others = []
        for d in steps:
            others.append(swap(kv, d))
        kv = sum(others, kv)
    other = swap(kv, 1)

    half = (size // 2, per_owner, 2 * channels)
    mode_shape = (per_owner, 2 * channels, channels)
    second, keep, send, w_near = pl.pallas_call(
        functools.partial(field_kernel, cells),
        out_shape=[
            pltpu.VMEM(field.shape, BF16),
            pltpu.VMEM(half, F32),
            pltpu.VMEM(half, BF16),
            pltpu.VMEM(mode_shape, BF16),
        ],
        grid_spec=pltpu.PrefetchScalarGridSpec(
            num_scalar_prefetch=1,
            grid=(strip_rows // ROWS,),
            in_specs=[HERE] * 9 + [hbm],
            out_specs=[HERE, HERE, HERE, HERE],
            scratch_shapes=[
                pltpu.VMEM((channels, channels), BF16),
                pltpu.VMEM((channels // 128, strip_rows * 2 * MW, 128), F32),
                pltpu.VMEM((channels // 64, MH * MW, 128), F32),
                pltpu.SemaphoreType.DMA(()),
            ],
        ),
        compiler_params=pltpu.CompilerParams(vmem_limit_bytes=14 << 20),
        name="field",
    )(ids, *map(near, (x_near, kv, other, queries, wa_near, wi_near, wo_near, wide, ahead)), away(w_modes.reshape(mode_shape)))

    both = (keep + swap(send, 1).astype(F32)).astype(BF16)
    terms = lax.all_to_all(both, "row", 0, 0, axis_index_groups=chips, tiled=True)

    group = 8
    copies = pl.pallas_call(
        mode_kernel,
        out_shape=pltpu.VMEM(half, BF16),
        grid=(per_owner // group,),
        in_specs=[HERE, HERE],
        out_specs=HERE,
        compiler_params=pltpu.CompilerParams(vmem_limit_bytes=4 << 20),
        name="modes",
    )(near(terms), near(w_near))

    held = lax.all_to_all(copies, "row", 0, 0, axis_index_groups=chips, tiled=True)
    far = swap(held, 1)

    return pl.pallas_call(
        functools.partial(last_kernel, cells),
        out_shape=jax.ShapeDtypeStruct(field.shape, BF16),
        grid_spec=pltpu.PrefetchScalarGridSpec(
            num_scalar_prefetch=1,
            grid=(strip_rows // LAST_ROWS,),
            in_specs=[HERE] * 6,
            out_specs=hbm,
            scratch_shapes=[
                pltpu.VMEM((channels // 64, MH * MW, 128), F32),
                pltpu.VMEM((channels // 128, strip_rows * 2 * MW, 128), F32),
                pltpu.VMEM(field.shape, BF16),
                pltpu.SemaphoreType.DMA((strip_rows, columns // LAST_SUB)),
            ],
        ),
        compiler_params=pltpu.CompilerParams(vmem_limit_bytes=12 << 20),
        name="last",
    )(ids, *map(near, (second, held, far, w_skip, tall, behind)))


def solution(mesh):
    placed = (P(("grp", "row"), None, None), P(), P(), P(), P(), P(), P("row", None, None, None))
    return jax.shard_map(local, mesh=mesh, in_specs=placed, out_specs=P(("grp", "row"), None, None), check_vma=False)
```
